32 devices in a mesh: tm: 16 (over z, y, core), space: 2 (over x).
Axes of the slice: x: 2, y: 2, z: 4, core: 2. Of those that a mesh axis runs over, the one named last changes fastest.
Arguments:
- queries: bfloat16 [32, 64, 3072], P('tm', 'space'), may hold values from -44 to 44
- keys: bfloat16 [32, 64, 3072], P('tm', 'space'), may hold values from -4 to 4
- values: bfloat16 [32, 64, 3072], P('tm', 'space'), may hold values from -24 to 24
- span_of_frame: int32 [32], replicated, may hold values from 0 to 15, never falling along the last dimension, each value on 1 to 4 neighbouring positions
Outputs:
- attended: bfloat16 [32, 64, 3072], P('tm', 'space')
The draws below stay inside these ranges and needn't reach their ends.
Inputs may be any that keep to these rules, and one draw needn't show every extreme that they name: `span_of_frame`: span indices never fall along the frames; each of the 16 spans holds 1 to 4 frames, and some span holds exactly 4.
All inputs are finite; a program needn't handle non-finite values.
Results may differ from the reference program's by a relative error of at most 0.005.
Values may be sent and summed in bfloat16 or wider, within the bound.
No kernel may reach another device: no remote copies, remote signals or barrier semaphores. Data moves between devices by JAX's collectives and lax.ppermute only.
A program may use at most 128 MiB of HBM per device.

```python
import math
import jax
import jax.numpy as jnp
import numpy as np
from jax import lax

HEADS = 24
HD = 128
SPANS = 16
FRAMES = 32
SPATIAL = 64
MOST = 4


def paired(key):
    key_q, key_k = jax.random.split(jax.random.fold_in(key, 7), 2)
    shape = (FRAMES, SPATIAL, HEADS * HD)
    query_all = 2.0 * jnp.clip(jax.random.normal(key_q, shape, jnp.float32), -3.0, 3.0)
    key_all = jnp.clip(jax.random.normal(key_k, shape, jnp.float32), -4.0, 4.0)
    return (query_all, key_all)


def draw_queries(key, part):
    return paired(key)[0].astype(jnp.bfloat16)


def draw_keys(key, part):
    return paired(key)[1].astype(jnp.bfloat16)


def steps_of(key, extent, pieces, least, high):
    gain = 1.0
    for position, shards_of in pieces:
        steps = jax.random.uniform(jax.random.fold_in(jax.random.fold_in(key, 6), position), (shards_of,), jnp.float32, least / len(pieces), high / len(pieces))
        gain = gain * jnp.repeat(jnp.exp(steps), extent[position] // shards_of).reshape((-1,) + (1,) * (len(extent) - 1 - position))
    return gain


def length_profile(amount, total, bound, slope):
    portions = [(1 << 20) // math.isqrt(grade ** slope) + 1 for grade in range(2, amount + 1)]
    spare, given = total - bound - (amount - 1), [1] * (amount - 1)
    while spare > 0:
        movable = [i for i in range(amount - 1) if given[i] < bound]
        whole, left = sum([portions[i] for i in movable]), spare
        for i in movable:
            more = min(bound - given[i], max(1, left * portions[i] // whole), spare)
            given[i] = given[i] + more
            spare = spare - more
    return np.array([bound] + given)


def uneven(rng, number_of, total, bound, slope):
    if number_of == 2:
        one = jax.random.randint(rng, (), max(1, total - bound), min(bound, total - 1) + 1)
        return jnp.stack([one, total - one])
    lengths = jnp.asarray(length_profile(number_of, total, bound, slope), jnp.int32)
    twos = (number_of - 1) // 2
    giver, sink = lengths[1:1 + 2 * twos:2], lengths[2:2 + 2 * twos:2]
    margin = jnp.minimum(giver - 1, bound - sink)
    moved = jax.random.randint(jax.random.fold_in(rng, 1), (twos,), 0, 1 << 20) % (margin + 1)
    lengths = lengths.at[1:1 + 2 * twos:2].set(giver - moved).at[2:2 + 2 * twos:2].set(sink + moved)
    return lengths[jax.random.permutation(jax.random.fold_in(rng, 2), number_of)]


def gaussian(key, shape, spread, reach, cuts=(), dtype=jnp.bfloat16):
    loudness = steps_of(key, shape, cuts, -0.22, 0.18) if cuts else 1.0
    result = jax.random.normal(key, shape, jnp.float32) * spread * loudness
    return jnp.minimum(jnp.maximum(result, -reach), reach).astype(dtype)


def setup_inputs(seed: int = 0) -> dict:
    streams_of = jax.random.split(jax.random.key(seed), 5)
    return {
        "queries": draw_queries(jax.random.fold_in(streams_of[4], 71), 0),
        "keys": draw_keys(jax.random.fold_in(streams_of[4], 71), 0),
        "values": gaussian(streams_of[2], (FRAMES, SPATIAL, HEADS * HD), 4.0, 24.0, ((0, 16), (1, 2))),
        "span_of_frame": jnp.searchsorted(jnp.cumsum(uneven(streams_of[3], SPANS, FRAMES, MOST, 2)), jnp.arange(FRAMES), side="right").astype(jnp.int32),
    }


def reference(queries, keys, values, span_of_frame):
    frames, spatial, width = queries.shape
    tokens = frames * spatial
    scale = HD ** -0.5
    key_span = jnp.repeat(span_of_frame, spatial)

    def one_head(head):
        offset = (head * HD).astype(jnp.int32)
        query_head = lax.dynamic_slice_in_dim(queries, offset, HD, 2)
        key_head = lax.dynamic_slice_in_dim(keys, offset, HD, 2).reshape(tokens, HD)
        value_head = lax.dynamic_slice_in_dim(values, offset, HD, 2).reshape(tokens, HD)

        def one_frame(frame):
            query_rows = lax.dynamic_index_in_dim(query_head, frame, 0, keepdims=False)
            scores = jnp.dot(query_rows, key_head.T, preferred_element_type=jnp.float32) * scale
            visible = key_span[None, :] <= span_of_frame[frame]
            peak = jnp.max(jnp.where(visible, scores, -jnp.inf), axis=1, keepdims=True)
            probs = jnp.where(visible, jnp.exp(scores - peak), 0.0)
            total = jnp.sum(probs, axis=1, keepdims=True)
            rounded = probs.astype(jnp.bfloat16)
            summed = jnp.dot(rounded, value_head, preferred_element_type=jnp.float32)
            return (summed / total).astype(jnp.bfloat16)

        return lax.map(one_frame, jnp.arange(frames).astype(jnp.int32))

    stacked = lax.map(one_head, jnp.arange(HEADS).astype(jnp.int32))
    return jnp.transpose(stacked, (1, 2, 0, 3)).reshape(frames, spatial, width)
```

```python
import functools
import math

import jax
import jax.numpy as jnp
from jax import lax
from jax.experimental import pallas as pl
from jax.experimental.pallas import tpu as pltpu
from jax.sharding import PartitionSpec as P

HD = 128
BLOCK = 256
VMEM = pl.BlockSpec(memory_space=pltpu.VMEM)
SMEM = pl.BlockSpec(memory_space=pltpu.SMEM)


def slots_of(heads, devices):
    return [head * devices // heads for head in range(heads)]


def pack_kernel(slots, q_ref, k_ref, v_ref, out_ref):
    rows = q_ref.shape[0]
    for head, slot in enumerate(slots):
        for place, ref in enumerate((q_ref, k_ref, v_ref)):
            out_ref[slot, place * rows : (place + 1) * rows, :] = ref[:, head * HD : (head + 1) * HD]


def unpack_kernel(slots, in_ref, out_ref):
    for head, slot in enumerate(slots):
        out_ref[:, head * HD : (head + 1) * HD] = in_ref[slot]


def attend_kernel(plan, span_ref, active_ref, x_ref, out_ref, score_ref, peak_ref, total_ref, sum_ref):
    sources, rows, spatial, group, per_frames = plan
    blocks = sources // group
    size = group * rows
    frames_dev = rows // spatial
    block_tms = max(1, group // per_frames)
    block_frames = block_tms * frames_dev
    scale = HD ** (-0.5) * math.log2(math.e)

    def first_frame(block):
        return (block * group) // per_frames * frames_dev

    def part(block, place):
        got = x_ref[pl.ds(block * group, group), place * rows : (place + 1) * rows, :]
        return got.reshape(size, HD)

    def spans_along(block, dimension, shape):
        at = lax.broadcasted_iota(jnp.int32, shape, dimension)
        local = (at // rows) // per_frames * frames_dev + (at % rows) // spatial
        base = first_frame(block)
        spans = jnp.full(shape, span_ref[base], jnp.int32)
        for frame in range(1, block_frames):
            spans = jnp.where(local == frame, span_ref[base + frame], spans)
        return spans

    def fold(values, op):
        got = values[:, :HD]
        for start in range(HD, values.shape[1], HD):
            got = op(got, values[:, start : start + HD])
        return got

    def scores_of(query, block):
        key = part(block, 1)
        return lax.dot_general(query, key, (((1,), (1,)), ((), ())), preferred_element_type=jnp.float32)

    def one_block(block, _):
        low = span_ref[first_frame(block)]
        high = span_ref[first_frame(block) + block_frames - 1]
        whole, seen = jnp.int32(0), jnp.int32(0)
        for other in range(blocks):
            start = first_frame(other)
            whole += (span_ref[start + block_frames - 1] <= low).astype(jnp.int32)
            seen += (span_ref[start] <= high).astype(jnp.int32)
        query = part(block, 0)
        peak_ref[...] = jnp.full_like(peak_ref, -jnp.inf)

        def plain(other, _):
            scores = scores_of(query, other)
            score_ref[other] = scores
            peak_ref[...] = jnp.maximum(peak_ref[...], fold(scores, jnp.maximum))
            return 0

        def masked(other, _):
            visible = spans_along(other, 1, (size, size)) <= spans_along(block, 0, (size, size))
            scores = jnp.where(visible, scores_of(query, other), -jnp.inf)
            score_ref[other] = scores
            peak_ref[...] = jnp.maximum(peak_ref[...], fold(scores, jnp.maximum))
            return 0

        lax.fori_loop(0, whole, plain, 0)
        lax.fori_loop(whole, seen, masked, 0)
        peak = jnp.max(peak_ref[...], axis=1, keepdims=True) * scale
        peak_ref[...] = jnp.broadcast_to(peak, peak_ref.shape)
        total_ref[...] = jnp.zeros_like(total_ref)
        sum_ref[...] = jnp.zeros_like(sum_ref)

        def weigh(other, _):
            peaks = jnp.concatenate([peak_ref[...]] * (size // HD), axis=1)
            probs = jnp.exp2(score_ref[other] * scale - peaks)
            total_ref[...] += fold(probs, jnp.add)
            sum_ref[...] += jnp.dot(probs.astype(jnp.bfloat16), part(other, 2), preferred_element_type=jnp.float32)
            return 0

        lax.fori_loop(0, seen, weigh, 0)
        total = jnp.sum(total_ref[...], axis=1, keepdims=True)
        result = (sum_ref[...] / total).astype(jnp.bfloat16)
        out_ref[pl.ds(block * group, group)] = result.reshape(group, rows, HD)
        return 0

    @pl.when(active_ref[0] == 1)
    def _():
        lax.fori_loop(0, blocks, one_block, 0)


def per_device(axes, sizes, queries, keys, values, span_of_frame):
    frames_here, spatial_here, width = queries.shape
    heads = width // HD
    rows = frames_here * spatial_here
    devices = math.prod(sizes)
    slots = slots_of(heads, devices)
    packed = pl.pallas_call(
        functools.partial(pack_kernel, slots),
        out_shape=jax.ShapeDtypeStruct((devices, 3 * rows, HD), jnp.bfloat16),
        in_specs=[VMEM] * 3,
        out_specs=VMEM,
    )(*(array.reshape(rows, width) for array in (queries, keys, values)))
    arrived = lax.all_to_all(packed, axes, split_axis=0, concat_axis=0, tiled=True)
    me = lax.axis_index(axes)
    active = functools.reduce(jnp.logical_or, [me == slot for slot in slots]).astype(jnp.int32)
    group = max(1, BLOCK // rows)
    size = group * rows
    plan = (devices, rows, spatial_here, group, sizes[1])
    result = pl.pallas_call(
        functools.partial(attend_kernel, plan),
        out_shape=jax.ShapeDtypeStruct((devices, rows, HD), jnp.bfloat16),
        in_specs=[SMEM, SMEM, VMEM],
        out_specs=VMEM,
        scratch_shapes=[
            pltpu.VMEM((devices // group, size, size), jnp.float32),
            pltpu.VMEM((size, HD), jnp.float32),
            pltpu.VMEM((size, HD), jnp.float32),
            pltpu.VMEM((size, HD), jnp.float32),
        ],
    )(span_of_frame, active.reshape(1), arrived)
    returned = lax.all_to_all(result, axes, split_axis=0, concat_axis=0, tiled=True)
    out = pl.pallas_call(
        functools.partial(unpack_kernel, slots),
        out_shape=jax.ShapeDtypeStruct((rows, width), jnp.bfloat16),
        in_specs=[VMEM],
        out_specs=VMEM,
    )(returned)
    return out.reshape(queries.shape)


def solution(mesh):
    axes = ("tm", "space")
    sizes = tuple(mesh.shape[axis] for axis in axes)
    return jax.shard_map(
        functools.partial(per_device, axes, sizes),
        mesh=mesh,
        in_specs=(P("tm", "space", None), P("tm", "space", None), P("tm", "space", None), P()),
        out_specs=P("tm", "space", None),
        check_vma=False,
    )
```

```python
import functools
import math

import jax
import jax.numpy as jnp
from jax import lax
from jax.experimental import pallas as pl
from jax.experimental.pallas import tpu as pltpu
from jax.sharding import PartitionSpec as P

HD = 128
BLOCK = 256
VMEM = pl.BlockSpec(memory_space=pltpu.VMEM)
SMEM = pl.BlockSpec(memory_space=pltpu.SMEM)


def slots_of(heads, devices):
    return [head * devices // heads for head in range(heads)]


def pack_kernel(slots, q_ref, k_ref, v_ref, out_ref):
    rows = q_ref.shape[0]
    for head, slot in enumerate(slots):
        for place, ref in enumerate((q_ref, k_ref, v_ref)):
            out_ref[slot, place * rows : (place + 1) * rows, :] = ref[:, head * HD : (head + 1) * HD]


def unpack_kernel(slots, in_ref, out_ref):
    for head, slot in enumerate(slots):
        out_ref[:, head * HD : (head + 1) * HD] = in_ref[slot]


def attend_kernel(plan, span_ref, active_ref, x_ref, out_ref, score_ref, peak_ref, total_ref, sum_ref):
    sources, rows, spatial, group, per_frames = plan
    blocks = sources // group
    size = group * rows
    frames_dev = rows // spatial
    block_tms = max(1, group // per_frames)
    block_frames = block_tms * frames_dev
    scale = HD ** (-0.5) * math.log2(math.e)

    def first_frame(block):
        return (block * group) // per_frames * frames_dev

    def part(block, place):
        got = x_ref[pl.ds(block * group, group), place * rows : (place + 1) * rows, :]
        return got.reshape(size, HD)

    def spans_along(block, dimension, shape):
        at = lax.broadcasted_iota(jnp.int32, shape, dimension)
        local = (at // rows) // per_frames * frames_dev + (at % rows) // spatial
        base = first_frame(block)
        spans = jnp.full(shape, span_ref[base], jnp.int32)
        for frame in range(1, block_frames):
            spans = jnp.where(local == frame, span_ref[base + frame], spans)
        return spans

    def fold(values, op):
        got = values[:, :HD]
        for start in range(HD, values.shape[1], HD):
            got = op(got, values[:, start : start + HD])
        return got

    def scores_of(query, block):
        key = part(block, 1)
        return lax.dot_general(query, key, (((1,), (1,)), ((), ())), preferred_element_type=jnp.float32)

    def one_block(block, _):
        low = span_ref[first_frame(block)]
        high = span_ref[first_frame(block) + block_frames - 1]
        whole, seen = jnp.int32(0), jnp.int32(0)
        for other in range(blocks):
            start = first_frame(other)
            whole += (span_ref[start + block_frames - 1] <= low).astype(jnp.int32)
            seen += (span_ref[start] <= high).astype(jnp.int32)
        query = part(block, 0)
        peak_ref[...] = jnp.full_like(peak_ref, -jnp.inf)

        def plain(other, _):
            scores = scores_of(query, other)
            score_ref[other] = scores
            peak_ref[...] = jnp.maximum(peak_ref[...], fold(scores, jnp.maximum))
            return 0

        def masked(other, _):
            visible = spans_along(other, 1, (size, size)) <= spans_along(block, 0, (size, size))
            scores = jnp.where(visible, scores_of(query, other), -jnp.inf)
            score_ref[other] = scores
            peak_ref[...] = jnp.maximum(peak_ref[...], fold(scores, jnp.maximum))
            return 0

        lax.fori_loop(0, whole, plain, 0)
        lax.fori_loop(whole, seen, masked, 0)
        peak = jnp.max(peak_ref[...], axis=1, keepdims=True) * scale
        peak_ref[...] = jnp.broadcast_to(peak, peak_ref.shape)
        total_ref[...] = jnp.zeros_like(total_ref)
        sum_ref[...] = jnp.zeros_like(sum_ref)

        def weigh(other, _):
            peaks = jnp.concatenate([peak_ref[...]] * (size // HD), axis=1)
            probs = jnp.exp2(score_ref[other] * scale - peaks)
            total_ref[...] += fold(probs, jnp.add)
            sum_ref[...] += jnp.dot(probs.astype(jnp.bfloat16), part(other, 2), preferred_element_type=jnp.float32)
            return 0

        lax.fori_loop(0, seen, weigh, 0)
        total = jnp.sum(total_ref[...], axis=1, keepdims=True)
        result = (sum_ref[...] / total).astype(jnp.bfloat16)
        out_ref[pl.ds(block * group, group)] = result.reshape(group, rows, HD)
        return 0

    @pl.when(active_ref[0] == 1)
    def _():
        lax.fori_loop(0, blocks, one_block, 0)


def halves_kernel(me_ref, q_ref, k_ref, v_ref, out_ref):
    rows, width = q_ref.shape
    half = width // 2
    start = pl.multiple_of((1 - me_ref[1]) * half, half)
    for place, ref in enumerate((q_ref, k_ref, v_ref)):
        out_ref[place * rows : (place + 1) * rows, :] = ref[:, pl.ds(start, half)]


def messages_kernel(pairs, me_ref, q_ref, k_ref, v_ref, other_ref, *out_refs):
    chips = len(out_refs)
    rows, width = q_ref.shape
    half = width // 2
    chip, core = me_ref[0], me_ref[1]
    for step, out_ref in enumerate(out_refs):
        to = chip ^ step
        pair = (to * pairs + chips - 1) // chips

        @pl.when((pair < pairs) & (pair * chips // pairs == to))
        def _(out_ref=out_ref, pair=pair):
            mine = pl.multiple_of(core * half + pair * HD, HD)
            theirs = pl.multiple_of(pair * HD, HD)
            for place, ref in enumerate((q_ref, k_ref, v_ref)):
                out_ref[place, pl.ds(pl.multiple_of(core * rows, rows), rows), :] = ref[:, pl.ds(mine, HD)]
                out_ref[place, pl.ds(pl.multiple_of((1 - core) * rows, rows), rows), :] = other_ref[
                    place * rows : (place + 1) * rows, pl.ds(theirs, HD)
                ]


def paired_kernel(plan, me_ref, span_ref, *refs):
    chips, space, rows, spatial = plan
    in_refs, (out_ref, x_ref, score_ref, peak_ref, total_ref, sum_ref, sems) = refs[:chips], refs[chips:]
    blocks = chips // space
    chip_rows = 2 * rows
    size = space * chip_rows
    frames_dev = rows // spatial
    block_frames = 2 * frames_dev
    scale = HD ** (-0.5) * math.log2(math.e)

    def part(block, place):
        return x_ref[block * space : (block + 1) * space, place].reshape(size, HD)

    def part_at(block, place):
        return x_ref[pl.ds(block * space, space), place].reshape(size, HD)

    def spans_along(block, dimension, shape):
        at = lax.broadcasted_iota(jnp.int32, shape, dimension)
        local = (at % chip_rows) // spatial
        spans = jnp.full(shape, span_ref[block * block_frames], jnp.int32)
        for frame in range(1, block_frames):
            spans = jnp.where(local == frame, span_ref[block * block_frames + frame], spans)
        return spans

    def fold(values, op):
        got = values[:, :HD]
        for start in range(HD, values.shape[1], HD):
            got = op(got, values[:, start : start + HD])
        return got

    def scores_of(query, key):
        return lax.dot_general(query, key, (((1,), (1,)), ((), ())), preferred_element_type=jnp.float32)

    def one_block(block):
        high = span_ref[(block + 1) * block_frames - 1]
        seen = jnp.int32(block + 1)
        for other in range(block + 1, blocks):
            seen += (span_ref[other * block_frames] <= high).astype(jnp.int32)
        query = part(block, 0)

        def masked(other, key):
            visible = spans_along(other, 1, (1, size)) <= spans_along(block, 0, (size, 1))
            return jnp.where(visible, scores_of(query, key), -jnp.inf)

        scores = masked(block, part(block, 1))
        score_ref[block] = scores
        top = fold(scores, jnp.maximum)
        for other in range(block):
            scores = scores_of(query, part(other, 1))
            score_ref[other] = scores
            top = jnp.maximum(top, fold(scores, jnp.maximum))
        peak_ref[...] = top

        def ahead(other, _):
            scores = masked(other, part_at(other, 1))
            score_ref[other] = scores
            peak_ref[...] = jnp.maximum(peak_ref[...], fold(scores, jnp.maximum))
            return 0

        lax.fori_loop(block + 1, seen, ahead, 0)
        peak = jnp.max(peak_ref[...], axis=1, keepdims=True) * scale

        def weigh(other, value):
            probs = jnp.exp2(score_ref[other] * scale - peak)
            weighed = jnp.dot(probs.astype(jnp.bfloat16), value, preferred_element_type=jnp.float32)
            return fold(probs, jnp.add), weighed

        total, weighed = weigh(0, part(0, 2))
        for other in range(1, block + 1):
            more_total, more = weigh(other, part(other, 2))
            total, weighed = total + more_total, weighed + more
        total_ref[...], sum_ref[...] = total, weighed

        def ahead_weigh(other, _):
            more_total, more = weigh(other, part_at(other, 2))
            total_ref[...] += more_total
            sum_ref[...] += more
            return 0

        lax.fori_loop(block + 1, seen, ahead_weigh, 0)
        total = jnp.sum(total_ref[...], axis=1, keepdims=True)
        result = (sum_ref[...] / total).astype(jnp.bfloat16)
        for place in range(space):
            for core in range(2):
                start = place * chip_rows + core * rows
                out_ref[(2 * block + core) * space + place] = result[start : start + rows]

    @pl.when(me_ref[2] == 1)
    def _():
        copies = [
            pltpu.make_async_copy(ref, x_ref.at[me_ref[0] ^ step], sems.at[step]) for step, ref in enumerate(in_refs)
        ]
        for copy in copies:
            copy.start()
        for copy in copies:
            copy.wait()
        for block in range(blocks):
            one_block(block)


def paired(axes, sizes, queries, keys, values, span_of_frame):
    frames_here, spatial_here, width = queries.shape
    heads = width // HD
    rows = frames_here * spatial_here
    space = sizes[1]
    devices = math.prod(sizes)
    chips, pairs = devices // 2, heads // 2
    held = slots_of(pairs, chips)

    def device(chip, core):
        return (2 * (chip // space) + core) * space + chip % space

    time, place = lax.axis_index(axes[0]), lax.axis_index(axes[1])
    chip, core = time // 2 * space + place, time % 2
    pair = (chip * pairs + chips - 1) // chips
    active = ((pair < pairs) & (pair * chips // pairs == chip)).astype(jnp.int32)
    me = jnp.stack([chip, core, active]).astype(jnp.int32)
    local = [array.reshape(rows, width) for array in (queries, keys, values)]
    half = pl.pallas_call(
        halves_kernel,
        out_shape=jax.ShapeDtypeStruct((3 * rows, width // 2), jnp.bfloat16),
        in_specs=[SMEM] + [VMEM] * 3,
        out_specs=VMEM,
    )(me, *local)
    across = [(device(c, core), device(c, 1 - core)) for c in range(chips) for core in range(2)]
    other = lax.ppermute(half, axes, across)
    messages = pl.pallas_call(
        functools.partial(messages_kernel, pairs),
        out_shape=[jax.ShapeDtypeStruct((3, 2 * rows, HD), jnp.bfloat16)] * chips,
        in_specs=[SMEM] + [VMEM] * 4,
        out_specs=[VMEM] * chips,
    )(me, *local, other)
    arrived = [messages[0]]
    for step in range(1, chips):
        hops = [(device(c, core), device(c ^ step, core)) for c in range(chips) if c ^ step in held for core in range(2)]
        arrived.append(lax.ppermute(messages[step], axes, hops))
    size = 2 * rows * space
    result = pl.pallas_call(
        functools.partial(paired_kernel, (chips, space, rows, spatial_here)),
        out_shape=jax.ShapeDtypeStruct((devices, rows, HD), jnp.bfloat16),
        in_specs=[SMEM, SMEM] + [pl.BlockSpec(memory_space=pl.ANY)] * chips,
        out_specs=VMEM,
        scratch_shapes=[
            pltpu.VMEM((chips, 3, 2 * rows, HD), jnp.bfloat16),
            pltpu.VMEM((chips // space, size, size), jnp.float32),
            pltpu.VMEM((size, HD), jnp.float32),
            pltpu.VMEM((size, HD), jnp.float32),
            pltpu.VMEM((size, HD), jnp.float32),
            pltpu.SemaphoreType.DMA((chips,)),
        ],
    )(me, span_of_frame, *arrived)
    returned = lax.all_to_all(result, axes, split_axis=0, concat_axis=0, tiled=True)
    slots = [device(chip, core) for core in range(2) for chip in held]
    out = pl.pallas_call(
        functools.partial(unpack_kernel, slots),
        out_shape=jax.ShapeDtypeStruct((rows, width), jnp.bfloat16),
        in_specs=[VMEM],
        out_specs=VMEM,
    )(returned)
    return out.reshape(queries.shape)


def per_device(axes, sizes, queries, keys, values, span_of_frame):
    chips, heads = math.prod(sizes) // 2, queries.shape[2] // HD
    fits = sizes[0] % 2 == 0 and heads % 2 == 0 and chips & (chips - 1) == 0
    way = paired if fits and heads // 2 <= chips <= heads else general
    return way(axes, sizes, queries, keys, values, span_of_frame)


def general(axes, sizes, queries, keys, values, span_of_frame):
    frames_here, spatial_here, width = queries.shape
    heads = width // HD
    rows = frames_here * spatial_here
    devices = math.prod(sizes)
    slots = slots_of(heads, devices)
    packed = pl.pallas_call(
        functools.partial(pack_kernel, slots),
        out_shape=jax.ShapeDtypeStruct((devices, 3 * rows, HD), jnp.bfloat16),
        in_specs=[VMEM] * 3,
        out_specs=VMEM,
    )(*(array.reshape(rows, width) for array in (queries, keys, values)))
    arrived = lax.all_to_all(packed, axes, split_axis=0, concat_axis=0, tiled=True)
    me = lax.axis_index(axes)
    active = functools.reduce(jnp.logical_or, [me == slot for slot in slots]).astype(jnp.int32)
    group = max(1, BLOCK // rows)
    size = group * rows
    plan = (devices, rows, spatial_here, group, sizes[1])
    result = pl.pallas_call(
        functools.partial(attend_kernel, plan),
        out_shape=jax.ShapeDtypeStruct((devices, rows, HD), jnp.bfloat16),
        in_specs=[SMEM, SMEM, VMEM],
        out_specs=VMEM,
        scratch_shapes=[
            pltpu.VMEM((devices // group, size, size), jnp.float32),
            pltpu.VMEM((size, HD), jnp.float32),
            pltpu.VMEM((size, HD), jnp.float32),
            pltpu.VMEM((size, HD), jnp.float32),
        ],
    )(span_of_frame, active.reshape(1), arrived)
    returned = lax.all_to_all(result, axes, split_axis=0, concat_axis=0, tiled=True)
    out = pl.pallas_call(
        functools.partial(unpack_kernel, slots),
        out_shape=jax.ShapeDtypeStruct((rows, width), jnp.bfloat16),
        in_specs=[VMEM],
        out_specs=VMEM,
    )(returned)
    return out.reshape(queries.shape)


def solution(mesh):
    axes = ("tm", "space")
    sizes = tuple(mesh.shape[axis] for axis in axes)
    return jax.shard_map(
        functools.partial(per_device, axes, sizes),
        mesh=mesh,
        in_specs=(P("tm", "space", None), P("tm", "space", None), P("tm", "space", None), P()),
        out_specs=P("tm", "space", None),
        check_vma=False,
    )
```

```python
import functools
import math

import jax
import jax.numpy as jnp
from jax import lax
from jax.experimental import pallas as pl
from jax.experimental.pallas import tpu as pltpu
from jax.sharding import PartitionSpec as P

HD = 128
BLOCK = 256
VMEM = pl.BlockSpec(memory_space=pltpu.VMEM)
SMEM = pl.BlockSpec(memory_space=pltpu.SMEM)


def slots_of(heads, devices):
    return [head * devices // heads for head in range(heads)]


def pack_kernel(slots, q_ref, k_ref, v_ref, out_ref):
    rows = q_ref.shape[0]
    for head, slot in enumerate(slots):
        for place, ref in enumerate((q_ref, k_ref, v_ref)):
            out_ref[slot, place * rows : (place + 1) * rows, :] = ref[:, head * HD : (head + 1) * HD]


def unpack_kernel(slots, in_ref, out_ref):
    for head, slot in enumerate(slots):
        out_ref[:, head * HD : (head + 1) * HD] = in_ref[slot]


def attend_kernel(plan, span_ref, active_ref, x_ref, out_ref, score_ref, peak_ref, total_ref, sum_ref):
    sources, rows, spatial, group, per_frames = plan
    blocks = sources // group
    size = group * rows
    frames_dev = rows // spatial
    block_tms = max(1, group // per_frames)
    block_frames = block_tms * frames_dev
    scale = HD ** (-0.5) * math.log2(math.e)

    def first_frame(block):
        return (block * group) // per_frames * frames_dev

    def part(block, place):
        got = x_ref[pl.ds(block * group, group), place * rows : (place + 1) * rows, :]
        return got.reshape(size, HD)

    def spans_along(block, dimension, shape):
        at = lax.broadcasted_iota(jnp.int32, shape, dimension)
        local = (at // rows) // per_frames * frames_dev + (at % rows) // spatial
        base = first_frame(block)
        spans = jnp.full(shape, span_ref[base], jnp.int32)
        for frame in range(1, block_frames):
            spans = jnp.where(local == frame, span_ref[base + frame], spans)
        return spans

    def fold(values, op):
        got = values[:, :HD]
        for start in range(HD, values.shape[1], HD):
            got = op(got, values[:, start : start + HD])
        return got

    def scores_of(query, block):
        key = part(block, 1)
        return lax.dot_general(query, key, (((1,), (1,)), ((), ())), preferred_element_type=jnp.float32)

    def one_block(block, _):
        low = span_ref[first_frame(block)]
        high = span_ref[first_frame(block) + block_frames - 1]
        whole, seen = jnp.int32(0), jnp.int32(0)
        for other in range(blocks):
            start = first_frame(other)
            whole += (span_ref[start + block_frames - 1] <= low).astype(jnp.int32)
            seen += (span_ref[start] <= high).astype(jnp.int32)
        query = part(block, 0)
        peak_ref[...] = jnp.full_like(peak_ref, -jnp.inf)

        def plain(other, _):
            scores = scores_of(query, other)
            score_ref[other] = scores
            peak_ref[...] = jnp.maximum(peak_ref[...], fold(scores, jnp.maximum))
            return 0

        def masked(other, _):
            visible = spans_along(other, 1, (size, size)) <= spans_along(block, 0, (size, size))
            scores = jnp.where(visible, scores_of(query, other), -jnp.inf)
            score_ref[other] = scores
            peak_ref[...] = jnp.maximum(peak_ref[...], fold(scores, jnp.maximum))
            return 0

        lax.fori_loop(0, whole, plain, 0)
        lax.fori_loop(whole, seen, masked, 0)
        peak = jnp.max(peak_ref[...], axis=1, keepdims=True) * scale
        peak_ref[...] = jnp.broadcast_to(peak, peak_ref.shape)
        total_ref[...] = jnp.zeros_like(total_ref)
        sum_ref[...] = jnp.zeros_like(sum_ref)

        def weigh(other, _):
            peaks = jnp.concatenate([peak_ref[...]] * (size // HD), axis=1)
            probs = jnp.exp2(score_ref[other] * scale - peaks)
            total_ref[...] += fold(probs, jnp.add)
            sum_ref[...] += jnp.dot(probs.astype(jnp.bfloat16), part(other, 2), preferred_element_type=jnp.float32)
            return 0

        lax.fori_loop(0, seen, weigh, 0)
        total = jnp.sum(total_ref[...], axis=1, keepdims=True)
        result = (sum_ref[...] / total).astype(jnp.bfloat16)
        out_ref[pl.ds(block * group, group)] = result.reshape(group, rows, HD)
        return 0

    @pl.when(active_ref[0] == 1)
    def _():
        lax.fori_loop(0, blocks, one_block, 0)


def unrolled_kernel(plan, span_ref, active_ref, x_ref, out_ref, score_ref, peak_ref, total_ref, sum_ref):
    sources, rows, spatial, group, per_frames = plan
    blocks = sources // group
    size = group * rows
    frames_dev = rows // spatial
    block_frames = max(1, group // per_frames) * frames_dev
    scale = HD ** (-0.5) * math.log2(math.e)

    def first_frame(block):
        return (block * group) // per_frames * frames_dev

    def part(block, place):
        return x_ref[pl.ds(block * group, group), place * rows : (place + 1) * rows, :].reshape(size, HD)

    def spans_along(block, dimension, shape):
        at = lax.broadcasted_iota(jnp.int32, shape, dimension)
        local = (at // rows) // per_frames * frames_dev + (at % rows) // spatial
        base = first_frame(block)
        spans = jnp.full(shape, span_ref[base], jnp.int32)
        for frame in range(1, block_frames):
            spans = jnp.where(local == frame, span_ref[base + frame], spans)
        return spans

    def fold(values, op):
        got = values[:, :HD]
        for start in range(HD, values.shape[1], HD):
            got = op(got, values[:, start : start + HD])
        return got

    def scores_of(query, key):
        return lax.dot_general(query, key, (((1,), (1,)), ((), ())), preferred_element_type=jnp.float32)

    def one_block(block):
        high = span_ref[first_frame(block) + block_frames - 1]
        seen = jnp.int32(block + 1)
        for other in range(block + 1, blocks):
            seen += (span_ref[first_frame(other)] <= high).astype(jnp.int32)
        query = part(block, 0)

        def masked(other):
            visible = spans_along(other, 1, (1, size)) <= spans_along(block, 0, (size, 1))
            return jnp.where(visible, scores_of(query, part(other, 1)), -jnp.inf)

        scores = masked(block)
        score_ref[block] = scores
        top = fold(scores, jnp.maximum)
        for other in range(block):
            scores = scores_of(query, part(other, 1))
            score_ref[other] = scores
            top = jnp.maximum(top, fold(scores, jnp.maximum))
        peak_ref[...] = top

        def ahead(other, _):
            scores = masked(other)
            score_ref[other] = scores
            peak_ref[...] = jnp.maximum(peak_ref[...], fold(scores, jnp.maximum))
            return 0

        lax.fori_loop(block + 1, seen, ahead, 0)
        peak = jnp.max(peak_ref[...], axis=1, keepdims=True) * scale

        def weigh(other):
            probs = jnp.exp2(score_ref[other] * scale - peak)
            weighed = jnp.dot(probs.astype(jnp.bfloat16), part(other, 2), preferred_element_type=jnp.float32)
            return fold(probs, jnp.add), weighed

        total, weighed = weigh(0)
        for other in range(1, block + 1):
            more_total, more = weigh(other)
            total, weighed = total + more_total, weighed + more
        total_ref[...], sum_ref[...] = total, weighed

        def ahead_weigh(other, _):
            more_total, more = weigh(other)
            total_ref[...] += more_total
            sum_ref[...] += more
            return 0

        lax.fori_loop(block + 1, seen, ahead_weigh, 0)
        total = jnp.sum(total_ref[...], axis=1, keepdims=True)
        result = (sum_ref[...] / total).astype(jnp.bfloat16)
        out_ref[block * group : (block + 1) * group] = result.reshape(group, rows, HD)

    @pl.when(active_ref[0] == 1)
    def _():
        for block in range(blocks):
            one_block(block)


def on_chip(axes, sizes, queries, keys, values, span_of_frame):
    frames_here, spatial_here, width = queries.shape
    heads = width // HD
    rows = frames_here * spatial_here
    devices = math.prod(sizes)
    slots = slots_of(heads, devices)
    me = lax.axis_index(axes)
    active = functools.reduce(jnp.logical_or, [me == slot for slot in slots]).astype(jnp.int32)
    local, active = lax.optimization_barrier(
        ([array.reshape(rows, width) for array in (queries, keys, values)], active.reshape(1))
    )
    packed = pl.pallas_call(
        functools.partial(pack_kernel, slots),
        out_shape=pltpu.VMEM((devices, 3 * rows, HD), jnp.bfloat16),
        in_specs=[VMEM] * 3,
        out_specs=VMEM,
    )(*local)
    arrived = lax.all_to_all(packed, axes, split_axis=0, concat_axis=0, tiled=True)
    group = max(1, BLOCK // rows)
    size = group * rows
    plan = (devices, rows, spatial_here, group, sizes[1])
    result = pl.pallas_call(
        functools.partial(unrolled_kernel, plan),
        out_shape=pltpu.VMEM((devices, rows, HD), jnp.bfloat16),
        in_specs=[SMEM, SMEM, VMEM],
        out_specs=VMEM,
        scratch_shapes=[
            pltpu.VMEM((devices // group, size, size), jnp.float32),
            pltpu.VMEM((size, HD), jnp.float32),
            pltpu.VMEM((size, HD), jnp.float32),
            pltpu.VMEM((size, HD), jnp.float32),
        ],
    )(span_of_frame, active, pltpu.with_memory_space_constraint(arrived, pltpu.VMEM))
    returned = lax.all_to_all(result, axes, split_axis=0, concat_axis=0, tiled=True)
    out = pl.pallas_call(
        functools.partial(unpack_kernel, slots),
        out_shape=jax.ShapeDtypeStruct((rows, width), jnp.bfloat16),
        in_specs=[VMEM],
        out_specs=VMEM,
    )(pltpu.with_memory_space_constraint(returned, pltpu.VMEM))
    return out.reshape(queries.shape)


def per_device(axes, sizes, queries, keys, values, span_of_frame):
    tokens = math.prod(sizes) * queries.shape[0] * queries.shape[1]
    way = on_chip if tokens <= 16 * BLOCK else general
    return way(axes, sizes, queries, keys, values, span_of_frame)


def general(axes, sizes, queries, keys, values, span_of_frame):
    frames_here, spatial_here, width = queries.shape
    heads = width // HD
    rows = frames_here * spatial_here
    devices = math.prod(sizes)
    slots = slots_of(heads, devices)
    packed = pl.pallas_call(
        functools.partial(pack_kernel, slots),
        out_shape=jax.ShapeDtypeStruct((devices, 3 * rows, HD), jnp.bfloat16),
        in_specs=[VMEM] * 3,
        out_specs=VMEM,
    )(*(array.reshape(rows, width) for array in (queries, keys, values)))
    arrived = lax.all_to_all(packed, axes, split_axis=0, concat_axis=0, tiled=True)
    me = lax.axis_index(axes)
    active = functools.reduce(jnp.logical_or, [me == slot for slot in slots]).astype(jnp.int32)
    group = max(1, BLOCK // rows)
    size = group * rows
    plan = (devices, rows, spatial_here, group, sizes[1])
    result = pl.pallas_call(
        functools.partial(attend_kernel, plan),
        out_shape=jax.ShapeDtypeStruct((devices, rows, HD), jnp.bfloat16),
        in_specs=[SMEM, SMEM, VMEM],
        out_specs=VMEM,
        scratch_shapes=[
            pltpu.VMEM((devices // group, size, size), jnp.float32),
            pltpu.VMEM((size, HD), jnp.float32),
            pltpu.VMEM((size, HD), jnp.float32),
            pltpu.VMEM((size, HD), jnp.float32),
        ],
    )(span_of_frame, active.reshape(1), arrived)
    returned = lax.all_to_all(result, axes, split_axis=0, concat_axis=0, tiled=True)
    out = pl.pallas_call(
        functools.partial(unpack_kernel, slots),
        out_shape=jax.ShapeDtypeStruct((rows, width), jnp.bfloat16),
        in_specs=[VMEM],
        out_specs=VMEM,
    )(returned)
    return out.reshape(queries.shape)


def solution(mesh):
    axes = ("tm", "space")
    sizes = tuple(mesh.shape[axis] for axis in axes)
    return jax.shard_map(
        functools.partial(per_device, axes, sizes),
        mesh=mesh,
        in_specs=(P("tm", "space", None), P("tm", "space", None), P("tm", "space", None), P()),
        out_specs=P("tm", "space", None),
        check_vma=False,
    )
```

```python
import functools
import math

import jax
import jax.numpy as jnp
from jax import lax
from jax.experimental import pallas as pl
from jax.experimental.pallas import tpu as pltpu
from jax.sharding import PartitionSpec as P

HD = 128
BLOCK = 256
VMEM = pl.BlockSpec(memory_space=pltpu.VMEM)
SMEM = pl.BlockSpec(memory_space=pltpu.SMEM)


def slots_of(heads, devices):
    return [head * devices // heads for head in range(heads)]


def pack_kernel(slots, q_ref, k_ref, v_ref, out_ref):
    rows = q_ref.shape[0]
    for head, slot in enumerate(slots):
        for place, ref in enumerate((q_ref, k_ref, v_ref)):
            out_ref[slot, place * rows : (place + 1) * rows, :] = ref[:, head * HD : (head + 1) * HD]


def unpack_kernel(slots, in_ref, out_ref):
    for head, slot in enumerate(slots):
        out_ref[:, head * HD : (head + 1) * HD] = in_ref[slot]


def attend_loops(plan, span_ref, x_ref, out_ref, score_ref, peak_ref, total_ref, sum_ref):
    sources, rows, spatial, group, per_frames = plan
    blocks = sources // group
    size = group * rows
    frames_dev = rows // spatial
    block_tms = max(1, group // per_frames)
    block_frames = block_tms * frames_dev
    scale = HD ** (-0.5) * math.log2(math.e)

    def first_frame(block):
        return (block * group) // per_frames * frames_dev

    def part(block, place):
        got = x_ref[pl.ds(block * group, group), place * rows : (place + 1) * rows, :]
        return got.reshape(size, HD)

    def spans_along(block, dimension, shape):
        at = lax.broadcasted_iota(jnp.int32, shape, dimension)
        local = (at // rows) // per_frames * frames_dev + (at % rows) // spatial
        base = first_frame(block)
        spans = jnp.full(shape, span_ref[base], jnp.int32)
        for frame in range(1, block_frames):
            spans = jnp.where(local == frame, span_ref[base + frame], spans)
        return spans

    def fold(values, op):
        got = values[:, :HD]
        for start in range(HD, values.shape[1], HD):
            got = op(got, values[:, start : start + HD])
        return got

    def scores_of(query, block):
        key = part(block, 1)
        return lax.dot_general(query, key, (((1,), (1,)), ((), ())), preferred_element_type=jnp.float32)

    def one_block(block, _):
        low = span_ref[first_frame(block)]
        high = span_ref[first_frame(block) + block_frames - 1]
        whole, seen = jnp.int32(0), jnp.int32(0)
        for other in range(blocks):
            start = first_frame(other)
            whole += (span_ref[start + block_frames - 1] <= low).astype(jnp.int32)
            seen += (span_ref[start] <= high).astype(jnp.int32)
        query = part(block, 0)
        peak_ref[...] = jnp.full_like(peak_ref, -jnp.inf)

        def plain(other, _):
            scores = scores_of(query, other)
            score_ref[other] = scores
            peak_ref[...] = jnp.maximum(peak_ref[...], fold(scores, jnp.maximum))
            return 0

        def masked(other, _):
            visible = spans_along(other, 1, (size, size)) <= spans_along(block, 0, (size, size))
            scores = jnp.where(visible, scores_of(query, other), -jnp.inf)
            score_ref[other] = scores
            peak_ref[...] = jnp.maximum(peak_ref[...], fold(scores, jnp.maximum))
            return 0

        lax.fori_loop(0, whole, plain, 0)
        lax.fori_loop(whole, seen, masked, 0)
        peak = jnp.max(peak_ref[...], axis=1, keepdims=True) * scale
        peak_ref[...] = jnp.broadcast_to(peak, peak_ref.shape)
        total_ref[...] = jnp.zeros_like(total_ref)
        sum_ref[...] = jnp.zeros_like(sum_ref)

        def weigh(other, _):
            peaks = jnp.concatenate([peak_ref[...]] * (size // HD), axis=1)
            probs = jnp.exp2(score_ref[other] * scale - peaks)
            total_ref[...] += fold(probs, jnp.add)
            sum_ref[...] += jnp.dot(probs.astype(jnp.bfloat16), part(other, 2), preferred_element_type=jnp.float32)
            return 0

        lax.fori_loop(0, seen, weigh, 0)
        total = jnp.sum(total_ref[...], axis=1, keepdims=True)
        result = (sum_ref[...] / total).astype(jnp.bfloat16)
        out_ref[pl.ds(block * group, group)] = result.reshape(group, rows, HD)
        return 0

    lax.fori_loop(0, blocks, one_block, 0)


def attend_kernel(plan, span_ref, active_ref, *refs):
    @pl.when(active_ref[0] == 1)
    def _():
        attend_loops(plan, span_ref, *refs)


def straight_kernel(plan, span_ref, active_ref, x_ref, out_ref, score_ref, peak_ref, total_ref, sum_ref):
    sources, rows, spatial, group, per_frames = plan
    blocks = sources // group
    size = group * rows
    frames_dev = rows // spatial
    block_frames = max(1, group // per_frames) * frames_dev
    scale = HD ** (-0.5) * math.log2(math.e)

    def first_frame(block):
        return (block * group) // per_frames * frames_dev

    def local_frame(row):
        return (row // rows) // per_frames * frames_dev + (row % rows) // spatial

    def part(block, place):
        return x_ref[block * group : (block + 1) * group, place * rows : (place + 1) * rows, :].reshape(size, HD)

    def fold(values, op):
        got = values[:, :HD]
        for start in range(HD, values.shape[1], HD):
            got = op(got, values[:, start : start + HD])
        return got

    def masked(scores, block, other):
        local = local_frame(lax.broadcasted_iota(jnp.int32, (1, size), 1))
        spans = jnp.full((1, size), span_ref[first_frame(other)], jnp.int32)
        for frame in range(1, block_frames):
            spans = jnp.where(local == frame, span_ref[first_frame(other) + frame], spans)
        pieces = []
        for start in range(0, size, spatial):
            mine = span_ref[first_frame(block) + local_frame(start)]
            pieces.append(jnp.where(spans <= mine, scores[start : start + spatial], -jnp.inf))
        return jnp.concatenate(pieces, axis=0)

    def seen(block):
        return range(min(block + 2, blocks))

    def make_scores(block):
        query, top = part(block, 0), None
        for other in seen(block):
            scores = lax.dot_general(
                query, part(other, 1), (((1,), (1,)), ((), ())), preferred_element_type=jnp.float32
            )
            if other >= block:
                scores = masked(scores, block, other)
            score_ref[block % 2, other] = scores
            folded = fold(scores, jnp.maximum)
            top = folded if top is None else jnp.maximum(top, folded)
        return jnp.max(top, axis=1, keepdims=True) * scale

    def weigh(block, peak):
        total = weighed = None
        for other in seen(block):
            probs = jnp.exp2(score_ref[block % 2, other] * scale - peak)
            folded = fold(probs, jnp.add)
            product = jnp.dot(probs.astype(jnp.bfloat16), part(other, 2), preferred_element_type=jnp.float32)
            total = folded if total is None else total + folded
            weighed = product if weighed is None else weighed + product
        result = weighed / jnp.sum(total, axis=1, keepdims=True)
        out_ref[block * group : (block + 1) * group] = result.astype(jnp.bfloat16).reshape(group, rows, HD)

    near = jnp.bool_(True)
    for block in range(blocks - 2):
        last = first_frame(block) + block_frames - 1
        near = near & (span_ref[first_frame(block + 2)] > span_ref[last])
    active = active_ref[0] == 1

    @pl.when(active & near)
    def _():
        peak = make_scores(0)
        for block in range(1, blocks):
            following = make_scores(block)
            weigh(block - 1, peak)
            peak = following
        weigh(blocks - 1, peak)

    @pl.when(active & jnp.logical_not(near))
    def _():
        attend_loops(plan, span_ref, x_ref, out_ref, score_ref.at[0], peak_ref, total_ref, sum_ref)


def on_chip(axes, sizes, queries, keys, values, span_of_frame):
    frames_here, spatial_here, width = queries.shape
    heads = width // HD
    rows = frames_here * spatial_here
    devices = math.prod(sizes)
    slots = slots_of(heads, devices)
    me = lax.axis_index(axes)
    active = functools.reduce(jnp.logical_or, [me == slot for slot in slots]).astype(jnp.int32)
    local, active = lax.optimization_barrier(
        ([array.reshape(rows, width) for array in (queries, keys, values)], active.reshape(1))
    )
    packed = pl.pallas_call(
        functools.partial(pack_kernel, slots),
        out_shape=pltpu.VMEM((devices, 3 * rows, HD), jnp.bfloat16),
        in_specs=[VMEM] * 3,
        out_specs=VMEM,
    )(*local)
    arrived = lax.all_to_all(packed, axes, split_axis=0, concat_axis=0, tiled=True)
    group = max(1, BLOCK // rows)
    size = group * rows
    plan = (devices, rows, spatial_here, group, sizes[1])
    result = pl.pallas_call(
        functools.partial(straight_kernel, plan),
        out_shape=pltpu.VMEM((devices, rows, HD), jnp.bfloat16),
        in_specs=[SMEM, SMEM, VMEM],
        out_specs=VMEM,
        scratch_shapes=[
            pltpu.VMEM((2, devices // group, size, size), jnp.float32),
            pltpu.VMEM((size, HD), jnp.float32),
            pltpu.VMEM((size, HD), jnp.float32),
            pltpu.VMEM((size, HD), jnp.float32),
        ],
    )(span_of_frame, active, pltpu.with_memory_space_constraint(arrived, pltpu.VMEM))
    returned = lax.all_to_all(result, axes, split_axis=0, concat_axis=0, tiled=True)
    out = pl.pallas_call(
        functools.partial(unpack_kernel, slots),
        out_shape=jax.ShapeDtypeStruct((rows, width), jnp.bfloat16),
        in_specs=[VMEM],
        out_specs=VMEM,
    )(pltpu.with_memory_space_constraint(returned, pltpu.VMEM))
    return out.reshape(queries.shape)


def per_device(axes, sizes, queries, keys, values, span_of_frame):
    tokens = math.prod(sizes) * queries.shape[0] * queries.shape[1]
    way = on_chip if tokens <= 16 * BLOCK else general
    return way(axes, sizes, queries, keys, values, span_of_frame)


def general(axes, sizes, queries, keys, values, span_of_frame):
    frames_here, spatial_here, width = queries.shape
    heads = width // HD
    rows = frames_here * spatial_here
    devices = math.prod(sizes)
    slots = slots_of(heads, devices)
    packed = pl.pallas_call(
        functools.partial(pack_kernel, slots),
        out_shape=jax.ShapeDtypeStruct((devices, 3 * rows, HD), jnp.bfloat16),
        in_specs=[VMEM] * 3,
        out_specs=VMEM,
    )(*(array.reshape(rows, width) for array in (queries, keys, values)))
    arrived = lax.all_to_all(packed, axes, split_axis=0, concat_axis=0, tiled=True)
    me = lax.axis_index(axes)
    active = functools.reduce(jnp.logical_or, [me == slot for slot in slots]).astype(jnp.int32)
    group = max(1, BLOCK // rows)
    size = group * rows
    plan = (devices, rows, spatial_here, group, sizes[1])
    result = pl.pallas_call(
        functools.partial(attend_kernel, plan),
        out_shape=jax.ShapeDtypeStruct((devices, rows, HD), jnp.bfloat16),
        in_specs=[SMEM, SMEM, VMEM],
        out_specs=VMEM,
        scratch_shapes=[
            pltpu.VMEM((devices // group, size, size), jnp.float32),
            pltpu.VMEM((size, HD), jnp.float32),
            pltpu.VMEM((size, HD), jnp.float32),
            pltpu.VMEM((size, HD), jnp.float32),
        ],
    )(span_of_frame, active.reshape(1), arrived)
    returned = lax.all_to_all(result, axes, split_axis=0, concat_axis=0, tiled=True)
    out = pl.pallas_call(
        functools.partial(unpack_kernel, slots),
        out_shape=jax.ShapeDtypeStruct((rows, width), jnp.bfloat16),
        in_specs=[VMEM],
        out_specs=VMEM,
    )(returned)
    return out.reshape(queries.shape)


def solution(mesh):
    axes = ("tm", "space")
    sizes = tuple(mesh.shape[axis] for axis in axes)
    return jax.shard_map(
        functools.partial(per_device, axes, sizes),
        mesh=mesh,
        in_specs=(P("tm", "space", None), P("tm", "space", None), P("tm", "space", None), P()),
        out_specs=P("tm", "space", None),
        check_vma=False,
    )
```

```python
import functools
import math

import jax
import jax.numpy as jnp
from jax import lax
from jax.experimental import pallas as pl
from jax.experimental.pallas import tpu as pltpu
from jax.sharding import PartitionSpec as P

HD = 128
BLOCK = 256
VMEM = pl.BlockSpec(memory_space=pltpu.VMEM)
SMEM = pl.BlockSpec(memory_space=pltpu.SMEM)


def slots_of(heads, devices):
    return [head * devices // heads for head in range(heads)]


def pack_kernel(slots, q_ref, k_ref, v_ref, out_ref):
    rows = q_ref.shape[0]
    for head, slot in enumerate(slots):
        for place, ref in enumerate((q_ref, k_ref, v_ref)):
            out_ref[slot, place * rows : (place + 1) * rows, :] = ref[:, head * HD : (head + 1) * HD]


def unpack_kernel(slots, in_ref, out_ref):
    for head, slot in enumerate(slots):
        out_ref[:, head * HD : (head + 1) * HD] = in_ref[slot]


def attend_loops(plan, span_ref, x_ref, out_ref, score_ref, peak_ref, total_ref, sum_ref):
    sources, rows, spatial, group, per_frames = plan
    blocks = sources // group
    size = group * rows
    frames_dev = rows // spatial
    block_tms = max(1, group // per_frames)
    block_frames = block_tms * frames_dev
    scale = HD ** (-0.5) * math.log2(math.e)

    def first_frame(block):
        return (block * group) // per_frames * frames_dev

    def part(block, place):
        got = x_ref[pl.ds(block * group, group), place * rows : (place + 1) * rows, :]
        return got.reshape(size, HD)

    def spans_along(block, dimension, shape):
        at = lax.broadcasted_iota(jnp.int32, shape, dimension)
        local = (at // rows) // per_frames * frames_dev + (at % rows) // spatial
        base = first_frame(block)
        spans = jnp.full(shape, span_ref[base], jnp.int32)
        for frame in range(1, block_frames):
            spans = jnp.where(local == frame, span_ref[base + frame], spans)
        return spans

    def fold(values, op):
        got = values[:, :HD]
        for start in range(HD, values.shape[1], HD):
            got = op(got, values[:, start : start + HD])
        return got

    def scores_of(query, block):
        key = part(block, 1)
        return lax.dot_general(query, key, (((1,), (1,)), ((), ())), preferred_element_type=jnp.float32)

    def one_block(block, _):
        low = span_ref[first_frame(block)]
        high = span_ref[first_frame(block) + block_frames - 1]
        whole, seen = jnp.int32(0), jnp.int32(0)
        for other in range(blocks):
            start = first_frame(other)
            whole += (span_ref[start + block_frames - 1] <= low).astype(jnp.int32)
            seen += (span_ref[start] <= high).astype(jnp.int32)
        query = part(block, 0)
        peak_ref[...] = jnp.full_like(peak_ref, -jnp.inf)

        def plain(other, _):
            scores = scores_of(query, other)
            score_ref[other] = scores
            peak_ref[...] = jnp.maximum(peak_ref[...], fold(scores, jnp.maximum))
            return 0

        def masked(other, _):
            visible = spans_along(other, 1, (size, size)) <= spans_along(block, 0, (size, size))
            scores = jnp.where(visible, scores_of(query, other), -jnp.inf)
            score_ref[other] = scores
            peak_ref[...] = jnp.maximum(peak_ref[...], fold(scores, jnp.maximum))
            return 0

        lax.fori_loop(0, whole, plain, 0)
        lax.fori_loop(whole, seen, masked, 0)
        peak = jnp.max(peak_ref[...], axis=1, keepdims=True) * scale
        peak_ref[...] = jnp.broadcast_to(peak, peak_ref.shape)
        total_ref[...] = jnp.zeros_like(total_ref)
        sum_ref[...] = jnp.zeros_like(sum_ref)

        def weigh(other, _):
            peaks = jnp.concatenate([peak_ref[...]] * (size // HD), axis=1)
            probs = jnp.exp2(score_ref[other] * scale - peaks)
            total_ref[...] += fold(probs, jnp.add)
            sum_ref[...] += jnp.dot(probs.astype(jnp.bfloat16), part(other, 2), preferred_element_type=jnp.float32)
            return 0

        lax.fori_loop(0, seen, weigh, 0)
        total = jnp.sum(total_ref[...], axis=1, keepdims=True)
        result = (sum_ref[...] / total).astype(jnp.bfloat16)
        out_ref[pl.ds(block * group, group)] = result.reshape(group, rows, HD)
        return 0

    lax.fori_loop(0, blocks, one_block, 0)


def attend_kernel(plan, span_ref, active_ref, *refs):
    @pl.when(active_ref[0] == 1)
    def _():
        attend_loops(plan, span_ref, *refs)


def straight_kernel(plan, span_ref, active_ref, x_ref, out_ref, score_ref, peak_ref, total_ref, sum_ref):
    sources, rows, spatial, group, per_frames = plan
    blocks = sources // group
    size = group * rows
    frames_dev = rows // spatial
    block_frames = max(1, group // per_frames) * frames_dev
    scale = HD ** (-0.5) * math.log2(math.e)

    def first_frame(block):
        return (block * group) // per_frames * frames_dev

    def local_frame(row):
        return (row // rows) // per_frames * frames_dev + (row % rows) // spatial

    def part(block, place):
        return x_ref[block * group : (block + 1) * group, place * rows : (place + 1) * rows, :].reshape(size, HD)

    def fold(values, op):
        got = values[:, :HD]
        for start in range(HD, values.shape[1], HD):
            got = op(got, values[:, start : start + HD])
        return got

    def masked(scores, block, other):
        local = local_frame(lax.broadcasted_iota(jnp.int32, (1, size), 1))
        spans = jnp.full((1, size), span_ref[first_frame(other)], jnp.int32)
        for frame in range(1, block_frames):
            spans = jnp.where(local == frame, span_ref[first_frame(other) + frame], spans)
        pieces = []
        for start in range(0, size, spatial):
            mine = span_ref[first_frame(block) + local_frame(start)]
            pieces.append(jnp.where(spans <= mine, scores[start : start + spatial], -jnp.inf))
        return jnp.concatenate(pieces, axis=0)

    def seen(block):
        return range(min(block + 2, blocks))

    def make_scores(block):
        query, top = part(block, 0), None
        for other in seen(block):
            scores = lax.dot_general(
                query, part(other, 1), (((1,), (1,)), ((), ())), preferred_element_type=jnp.float32
            )
            if other >= block:
                scores = masked(scores, block, other)
            score_ref[block % 2, other] = scores
            folded = fold(scores, jnp.maximum)
            top = folded if top is None else jnp.maximum(top, folded)
        return jnp.max(top, axis=1, keepdims=True) * scale

    def weigh(block, peak):
        total = weighed = None
        for other in seen(block):
            probs = jnp.exp2(score_ref[block % 2, other] * scale - peak)
            folded = fold(probs, jnp.add)
            product = jnp.dot(probs.astype(jnp.bfloat16), part(other, 2), preferred_element_type=jnp.float32)
            total = folded if total is None else total + folded
            weighed = product if weighed is None else weighed + product
        result = weighed / jnp.sum(total, axis=1, keepdims=True)
        out_ref[block * group : (block + 1) * group] = result.astype(jnp.bfloat16).reshape(group, rows, HD)

    near = jnp.bool_(True)
    for block in range(blocks - 2):
        last = first_frame(block) + block_frames - 1
        near = near & (span_ref[first_frame(block + 2)] > span_ref[last])
    active = active_ref[0] == 1

    @pl.when(active & near)
    def _():
        peak = make_scores(0)
        for block in range(1, blocks):
            following = make_scores(block)
            weigh(block - 1, peak)
            peak = following
        weigh(blocks - 1, peak)

    @pl.when(active & jnp.logical_not(near))
    def _():
        attend_loops(plan, span_ref, x_ref, out_ref, score_ref.at[0], peak_ref, total_ref, sum_ref)


def on_chip(axes, sizes, queries, keys, values, span_of_frame):
    frames_here, spatial_here, width = queries.shape
    heads = width // HD
    rows = frames_here * spatial_here
    devices = math.prod(sizes)
    slots = slots_of(heads, devices)
    me = lax.axis_index(axes)
    active = functools.reduce(jnp.logical_or, [me == slot for slot in slots]).astype(jnp.int32)
    local, active = lax.optimization_barrier(
        ([array.reshape(rows, width) for array in (queries, keys, values)], active.reshape(1))
    )
    packed = pl.pallas_call(
        functools.partial(pack_kernel, slots),
        out_shape=pltpu.VMEM((devices, 3 * rows, HD), jnp.bfloat16),
        in_specs=[VMEM] * 3,
        out_specs=VMEM,
    )(*local)
    arrived = lax.all_to_all(packed, axes, split_axis=0, concat_axis=0, tiled=True)
    group = max(1, BLOCK // rows)
    size = group * rows
    plan = (devices, rows, spatial_here, group, sizes[1])
    result = pl.pallas_call(
        functools.partial(straight_kernel, plan),
        out_shape=pltpu.VMEM((devices, rows, HD), jnp.bfloat16),
        in_specs=[SMEM, SMEM, VMEM],
        out_specs=VMEM,
        scratch_shapes=[
            pltpu.VMEM((2, devices // group, size, size), jnp.float32),
            pltpu.VMEM((size, HD), jnp.float32),
            pltpu.VMEM((size, HD), jnp.float32),
            pltpu.VMEM((size, HD), jnp.float32),
        ],
    )(span_of_frame, active, pltpu.with_memory_space_constraint(arrived, pltpu.VMEM))
    returned = lax.all_to_all(result, axes, split_axis=0, concat_axis=0, tiled=True)
    out = pl.pallas_call(
        functools.partial(unpack_kernel, slots),
        out_shape=jax.ShapeDtypeStruct((rows, width), jnp.bfloat16),
        in_specs=[VMEM],
        out_specs=VMEM,
    )(pltpu.with_memory_space_constraint(returned, pltpu.VMEM))
    return out.reshape(queries.shape)


def shared_pack_kernel(q_ref, k_ref, v_ref, out_ref):
    rows = q_ref.shape[0]
    half, kept = rows // 2, rows - rows // 4

    def of(ref, head, start=0, stop=rows):
        return ref[start:stop, head * HD : (head + 1) * HD]

    for time in range(0, out_ref.shape[0] // 2, 2):
        for place in range(2):
            own, both = time // 2 * 3 + 2 * place, time // 2 * 3 + 1
            for slot, head in ((time * 2 + place, own), (time * 2 + 2 + place, both)):
                out_ref[slot, :rows] = of(k_ref, head)
                out_ref[slot, rows : 2 * rows] = of(v_ref, head)
            out_ref[time * 2 + place, 2 * rows :] = of(q_ref, own, 0, kept)
            out_ref[time * 2 + 2 + place, 2 * rows : 2 * rows + half] = of(q_ref, both, place * half, (place + 1) * half)
            out_ref[time * 2 + 2 + place, 2 * rows + half :] = of(q_ref, own, kept, rows)


def shared_unpack_kernel(in_ref, out_ref):
    rows = out_ref.shape[0]
    half = rows // 2
    for time in range(0, in_ref.shape[0] // 2, 2):
        for place in range(2):
            own, both = time // 2 * 3 + 2 * place, time // 2 * 3 + 1
            out_ref[:, own * HD : (own + 1) * HD] = in_ref[time * 2 + place]
            out_ref[place * half : (place + 1) * half, both * HD : (both + 1) * HD] = in_ref[time * 2 + 2 + place, :half]


def shared_kernel(plan, span_ref, me_ref, x_ref, rest_ref, out_ref, score_ref, peak_ref, total_ref, sum_ref):
    devices, rows, spatial, group = plan
    blocks = devices // group
    size = group * rows
    half = rows // 2
    block_frames = group // 2 * (rows // spatial)
    scale = HD ** (-0.5) * math.log2(math.e)

    def local_frame(row):
        return row // (2 * rows) * (rows // spatial) + row % rows // spatial

    def part(block, place):
        got = x_ref[pl.ds(block * group, group), place * rows : (place + 1) * rows, :]
        return got.reshape(size, HD)

    def fold(values, op):
        got = values[:, :HD]
        for start in range(HD, values.shape[1], HD):
            got = op(got, values[:, start : start + HD])
        return got

    def scores_of(query, other, mine):
        key = part(other, 0)
        scores = lax.dot_general(query, key, (((1,), (1,)), ((), ())), preferred_element_type=jnp.float32)
        if mine is None:
            return scores
        local = local_frame(lax.broadcasted_iota(jnp.int32, (1, size), 1))
        spans = jnp.full((1, size), span_ref[other * block_frames], jnp.int32)
        for frame in range(1, block_frames):
            spans = jnp.where(local == frame, span_ref[other * block_frames + frame], spans)
        pieces = []
        for start in range(0, size, spatial):
            pieces.append(jnp.where(spans <= mine(start), scores[start : start + spatial], -jnp.inf))
        return jnp.concatenate(pieces, axis=0)

    def probs_of(slot, other, peak):
        probs = jnp.exp2(score_ref[slot, other] * scale - peak)
        product = jnp.dot(probs.astype(jnp.bfloat16), part(other, 1), preferred_element_type=jnp.float32)
        return fold(probs, jnp.add), product

    def straight(wide, query_of, mine_of, write):
        tiles = blocks // wide

        def seen(tile):
            return range(min((tile + 1) * wide + 1, blocks))

        def make_scores(tile):
            query, top = query_of(tile), None
            for other in seen(tile):
                scores = scores_of(query, other, mine_of(tile) if other >= tile * wide else None)
                score_ref[tile % 2, other] = scores
                folded = fold(scores, jnp.maximum)
                top = folded if top is None else jnp.maximum(top, folded)
            return jnp.max(top, axis=1, keepdims=True) * scale

        def weigh(tile, peak):
            total = weighed = None
            for other in seen(tile):
                folded, product = probs_of(tile % 2, other, peak)
                total = folded if total is None else total + folded
                weighed = product if weighed is None else weighed + product
            write(tile, (weighed / jnp.sum(total, axis=1, keepdims=True)).astype(jnp.bfloat16))

        peak = make_scores(0)
        for tile in range(1, tiles):
            following = make_scores(tile)
            weigh(tile - 1, peak)
            peak = following
        weigh(tiles - 1, peak)

    def looped(wide, query_of, mine_of, write):
        for tile in range(blocks // wide):
            query, mine = query_of(tile), mine_of(tile)
            peak_ref[...] = jnp.full_like(peak_ref, -jnp.inf)
            total_ref[...] = jnp.zeros_like(total_ref)
            sum_ref[...] = jnp.zeros_like(sum_ref)

            def score(other, _, query=query, mine=mine):
                scores = scores_of(query, other, mine)
                score_ref[0, other] = scores
                peak_ref[...] = jnp.maximum(peak_ref[...], fold(scores, jnp.maximum))
                return 0

            lax.fori_loop(0, blocks, score, 0)
            peak = jnp.max(peak_ref[...], axis=1, keepdims=True) * scale

            def weigh(other, _, peak=peak):
                folded, product = probs_of(0, other, peak)
                total_ref[...] += folded
                sum_ref[...] += product
                return 0

            lax.fori_loop(0, blocks, weigh, 0)
            write(tile, (sum_ref[...] / jnp.sum(total_ref[...], axis=1, keepdims=True)).astype(jnp.bfloat16))

    def own_query(tile):
        sources = pl.ds(tile * group, group)
        return jnp.concatenate([x_ref[sources, 2 * rows :, :], rest_ref[sources]], axis=1).reshape(size, HD)

    def own_span(tile):
        return lambda start: span_ref[tile * block_frames + local_frame(start)]

    def own_write(tile, result):
        out_ref[pl.ds(tile * group, group)] = result.reshape(group, rows, HD)

    def both_query(tile):
        return x_ref[pl.ds(tile * 2 * group, 2 * group), 2 * rows : 2 * rows + half, :].reshape(size, HD)

    def both_span(tile):
        return lambda start: span_ref[(tile * 2 * group + start // half) // 2 * 2 + me_ref[1]]

    def both_write(tile, result):
        out_ref[pl.ds(tile * 2 * group, 2 * group), :half, :] = result.reshape(2 * group, half, HD)

    near = jnp.bool_(True)
    for block in range(blocks - 2):
        near = near & (span_ref[(block + 2) * block_frames] > span_ref[(block + 1) * block_frames - 1])
    for core, roles in enumerate(((1, own_query, own_span, own_write), (2, both_query, both_span, both_write))):
        here = me_ref[0] == core
        pl.when(here & near)(functools.partial(straight, *roles))
        pl.when(here & jnp.logical_not(near))(functools.partial(looped, *roles))


def shared(axes, sizes, queries, keys, values, span_of_frame):
    frames_here, spatial_here, width = queries.shape
    rows = frames_here * spatial_here
    devices = math.prod(sizes)
    group = BLOCK // rows
    size = group * rows
    me = jnp.stack([lax.axis_index(axes[0]) % 2, lax.axis_index(axes[1])]).astype(jnp.int32)
    local, me = lax.optimization_barrier(([array.reshape(rows, width) for array in (queries, keys, values)], me))
    kept = rows - rows // 4
    packed = pl.pallas_call(
        shared_pack_kernel,
        out_shape=pltpu.VMEM((devices, 2 * rows + kept, HD), jnp.bfloat16),
        in_specs=[VMEM] * 3,
        out_specs=VMEM,
    )(*local)
    arrived = lax.all_to_all(packed, axes, split_axis=0, concat_axis=0, tiled=True)
    across = [(device, device ^ sizes[1]) for device in range(devices)]
    rest = lax.ppermute(arrived[:, 2 * rows + rows // 2 :], axes, across)
    result = pl.pallas_call(
        functools.partial(shared_kernel, (devices, rows, spatial_here, group)),
        out_shape=pltpu.VMEM((devices, rows, HD), jnp.bfloat16),
        in_specs=[SMEM, SMEM, VMEM, VMEM],
        out_specs=VMEM,
        scratch_shapes=[
            pltpu.VMEM((2, devices // group, size, size), jnp.float32),
            pltpu.VMEM((size, HD), jnp.float32),
            pltpu.VMEM((size, HD), jnp.float32),
            pltpu.VMEM((size, HD), jnp.float32),
        ],
    )(
        span_of_frame,
        me,
        pltpu.with_memory_space_constraint(arrived, pltpu.VMEM),
        pltpu.with_memory_space_constraint(rest, pltpu.VMEM),
    )
    returned = lax.all_to_all(result, axes, split_axis=0, concat_axis=0, tiled=True)
    out = pl.pallas_call(
        shared_unpack_kernel,
        out_shape=jax.ShapeDtypeStruct((rows, width), jnp.bfloat16),
        in_specs=[VMEM],
        out_specs=VMEM,
    )(pltpu.with_memory_space_constraint(returned, pltpu.VMEM))
    return out.reshape(queries.shape)


def per_device(axes, sizes, queries, keys, values, span_of_frame):
    tokens = math.prod(sizes) * queries.shape[0] * queries.shape[1]
    way = on_chip if tokens <= 16 * BLOCK else general
    frames_here, spatial_here, width = queries.shape
    fits = sizes[1] == 2 and sizes[0] % 2 == 0 and 2 * (width // HD) == 3 * sizes[0] and frames_here == 2
    if way is on_chip and fits and spatial_here % 32 == 0 and BLOCK % (4 * spatial_here) == 0:
        way = shared
    return way(axes, sizes, queries, keys, values, span_of_frame)


def general(axes, sizes, queries, keys, values, span_of_frame):
    frames_here, spatial_here, width = queries.shape
    heads = width // HD
    rows = frames_here * spatial_here
    devices = math.prod(sizes)
    slots = slots_of(heads, devices)
    packed = pl.pallas_call(
        functools.partial(pack_kernel, slots),
        out_shape=jax.ShapeDtypeStruct((devices, 3 * rows, HD), jnp.bfloat16),
        in_specs=[VMEM] * 3,
        out_specs=VMEM,
    )(*(array.reshape(rows, width) for array in (queries, keys, values)))
    arrived = lax.all_to_all(packed, axes, split_axis=0, concat_axis=0, tiled=True)
    me = lax.axis_index(axes)
    active = functools.reduce(jnp.logical_or, [me == slot for slot in slots]).astype(jnp.int32)
    group = max(1, BLOCK // rows)
    size = group * rows
    plan = (devices, rows, spatial_here, group, sizes[1])
    result = pl.pallas_call(
        functools.partial(attend_kernel, plan),
        out_shape=jax.ShapeDtypeStruct((devices, rows, HD), jnp.bfloat16),
        in_specs=[SMEM, SMEM, VMEM],
        out_specs=VMEM,
        scratch_shapes=[
            pltpu.VMEM((devices // group, size, size), jnp.float32),
            pltpu.VMEM((size, HD), jnp.float32),
            pltpu.VMEM((size, HD), jnp.float32),
            pltpu.VMEM((size, HD), jnp.float32),
        ],
    )(span_of_frame, active.reshape(1), arrived)
    returned = lax.all_to_all(result, axes, split_axis=0, concat_axis=0, tiled=True)
    out = pl.pallas_call(
        functools.partial(unpack_kernel, slots),
        out_shape=jax.ShapeDtypeStruct((rows, width), jnp.bfloat16),
        in_specs=[VMEM],
        out_specs=VMEM,
    )(returned)
    return out.reshape(queries.shape)


def solution(mesh):
    axes = ("tm", "space")
    sizes = tuple(mesh.shape[axis] for axis in axes)
    return jax.shard_map(
        functools.partial(per_device, axes, sizes),
        mesh=mesh,
        in_specs=(P("tm", "space", None), P("tm", "space", None), P("tm", "space", None), P()),
        out_specs=P("tm", "space", None),
        check_vma=False,
    )
```

```python
import functools
import math

import jax
import jax.numpy as jnp
from jax import lax
from jax.experimental import pallas as pl
from jax.experimental.pallas import tpu as pltpu
from jax.sharding import PartitionSpec as P

HD = 128
BLOCK = 256
VMEM = pl.BlockSpec(memory_space=pltpu.VMEM)
SMEM = pl.BlockSpec(memory_space=pltpu.SMEM)


def slots_of(heads, devices):
    return [head * devices // heads for head in range(heads)]


def pack_kernel(slots, q_ref, k_ref, v_ref, out_ref):
    rows = q_ref.shape[0]
    for head, slot in enumerate(slots):
        for place, ref in enumerate((q_ref, k_ref, v_ref)):
            out_ref[slot, place * rows : (place + 1) * rows, :] = ref[:, head * HD : (head + 1) * HD]


def unpack_kernel(slots, in_ref, out_ref):
    for head, slot in enumerate(slots):
        out_ref[:, head * HD : (head + 1) * HD] = in_ref[slot]


def attend_loops(plan, span_ref, x_ref, out_ref, score_ref, peak_ref, total_ref, sum_ref):
    sources, rows, spatial, group, per_frames = plan
    blocks = sources // group
    size = group * rows
    frames_dev = rows // spatial
    block_tms = max(1, group // per_frames)
    block_frames = block_tms * frames_dev
    scale = HD ** (-0.5) * math.log2(math.e)

    def first_frame(block):
        return (block * group) // per_frames * frames_dev

    def part(block, place):
        got = x_ref[pl.ds(block * group, group), place * rows : (place + 1) * rows, :]
        return got.reshape(size, HD)

    def spans_along(block, dimension, shape):
        at = lax.broadcasted_iota(jnp.int32, shape, dimension)
        local = (at // rows) // per_frames * frames_dev + (at % rows) // spatial
        base = first_frame(block)
        spans = jnp.full(shape, span_ref[base], jnp.int32)
        for frame in range(1, block_frames):
            spans = jnp.where(local == frame, span_ref[base + frame], spans)
        return spans

    def fold(values, op):
        got = values[:, :HD]
        for start in range(HD, values.shape[1], HD):
            got = op(got, values[:, start : start + HD])
        return got

    def scores_of(query, block):
        key = part(block, 1)
        return lax.dot_general(query, key, (((1,), (1,)), ((), ())), preferred_element_type=jnp.float32)

    def one_block(block, _):
        low = span_ref[first_frame(block)]
        high = span_ref[first_frame(block) + block_frames - 1]
        whole, seen = jnp.int32(0), jnp.int32(0)
        for other in range(blocks):
            start = first_frame(other)
            whole += (span_ref[start + block_frames - 1] <= low).astype(jnp.int32)
            seen += (span_ref[start] <= high).astype(jnp.int32)
        query = part(block, 0)
        peak_ref[...] = jnp.full_like(peak_ref, -jnp.inf)

        def plain(other, _):
            scores = scores_of(query, other)
            score_ref[other] = scores
            peak_ref[...] = jnp.maximum(peak_ref[...], fold(scores, jnp.maximum))
            return 0

        def masked(other, _):
            visible = spans_along(other, 1, (size, size)) <= spans_along(block, 0, (size, size))
            scores = jnp.where(visible, scores_of(query, other), -jnp.inf)
            score_ref[other] = scores
            peak_ref[...] = jnp.maximum(peak_ref[...], fold(scores, jnp.maximum))
            return 0

        lax.fori_loop(0, whole, plain, 0)
        lax.fori_loop(whole, seen, masked, 0)
        peak = jnp.max(peak_ref[...], axis=1, keepdims=True) * scale
        peak_ref[...] = jnp.broadcast_to(peak, peak_ref.shape)
        total_ref[...] = jnp.zeros_like(total_ref)
        sum_ref[...] = jnp.zeros_like(sum_ref)

        def weigh(other, _):
            peaks = jnp.concatenate([peak_ref[...]] * (size // HD), axis=1)
            probs = jnp.exp2(score_ref[other] * scale - peaks)
            total_ref[...] += fold(probs, jnp.add)
            sum_ref[...] += jnp.dot(probs.astype(jnp.bfloat16), part(other, 2), preferred_element_type=jnp.float32)
            return 0

        lax.fori_loop(0, seen, weigh, 0)
        total = jnp.sum(total_ref[...], axis=1, keepdims=True)
        result = (sum_ref[...] / total).astype(jnp.bfloat16)
        out_ref[pl.ds(block * group, group)] = result.reshape(group, rows, HD)
        return 0

    lax.fori_loop(0, blocks, one_block, 0)


def attend_kernel(plan, span_ref, active_ref, *refs):
    @pl.when(active_ref[0] == 1)
    def _():
        attend_loops(plan, span_ref, *refs)


def straight_kernel(plan, span_ref, active_ref, x_ref, out_ref, score_ref, peak_ref, total_ref, sum_ref):
    sources, rows, spatial, group, per_frames = plan
    blocks = sources // group
    size = group * rows
    frames_dev = rows // spatial
    block_frames = max(1, group // per_frames) * frames_dev
    scale = HD ** (-0.5) * math.log2(math.e)

    def first_frame(block):
        return (block * group) // per_frames * frames_dev

    def local_frame(row):
        return (row // rows) // per_frames * frames_dev + (row % rows) // spatial

    def part(block, place):
        return x_ref[block * group : (block + 1) * group, place * rows : (place + 1) * rows, :].reshape(size, HD)

    def fold(values, op):
        got = values[:, :HD]
        for start in range(HD, values.shape[1], HD):
            got = op(got, values[:, start : start + HD])
        return got

    def masked(scores, block, other):
        local = local_frame(lax.broadcasted_iota(jnp.int32, (1, size), 1))
        spans = jnp.full((1, size), span_ref[first_frame(other)], jnp.int32)
        for frame in range(1, block_frames):
            spans = jnp.where(local == frame, span_ref[first_frame(other) + frame], spans)
        pieces = []
        for start in range(0, size, spatial):
            mine = span_ref[first_frame(block) + local_frame(start)]
            pieces.append(jnp.where(spans <= mine, scores[start : start + spatial], -jnp.inf))
        return jnp.concatenate(pieces, axis=0)

    def seen(block):
        return range(min(block + 2, blocks))

    def make_scores(block):
        query, top = part(block, 0), None
        for other in seen(block):
            scores = lax.dot_general(
                query, part(other, 1), (((1,), (1,)), ((), ())), preferred_element_type=jnp.float32
            )
            if other >= block:
                scores = masked(scores, block, other)
            score_ref[block % 2, other] = scores
            folded = fold(scores, jnp.maximum)
            top = folded if top is None else jnp.maximum(top, folded)
        return jnp.max(top, axis=1, keepdims=True) * scale

    def weigh(block, peak):
        total = weighed = None
        for other in seen(block):
            probs = jnp.exp2(score_ref[block % 2, other] * scale - peak)
            folded = fold(probs, jnp.add)
            product = jnp.dot(probs.astype(jnp.bfloat16), part(other, 2), preferred_element_type=jnp.float32)
            total = folded if total is None else total + folded
            weighed = product if weighed is None else weighed + product
        result = weighed / jnp.sum(total, axis=1, keepdims=True)
        out_ref[block * group : (block + 1) * group] = result.astype(jnp.bfloat16).reshape(group, rows, HD)

    near = jnp.bool_(True)
    for block in range(blocks - 2):
        last = first_frame(block) + block_frames - 1
        near = near & (span_ref[first_frame(block + 2)] > span_ref[last])
    active = active_ref[0] == 1

    @pl.when(active & near)
    def _():
        peak = make_scores(0)
        for block in range(1, blocks):
            following = make_scores(block)
            weigh(block - 1, peak)
            peak = following
        weigh(blocks - 1, peak)

    @pl.when(active & jnp.logical_not(near))
    def _():
        attend_loops(plan, span_ref, x_ref, out_ref, score_ref.at[0], peak_ref, total_ref, sum_ref)


def on_chip(axes, sizes, queries, keys, values, span_of_frame):
    frames_here, spatial_here, width = queries.shape
    heads = width // HD
    rows = frames_here * spatial_here
    devices = math.prod(sizes)
    slots = slots_of(heads, devices)
    me = lax.axis_index(axes)
    active = functools.reduce(jnp.logical_or, [me == slot for slot in slots]).astype(jnp.int32)
    local, active = lax.optimization_barrier(
        ([array.reshape(rows, width) for array in (queries, keys, values)], active.reshape(1))
    )
    packed = pl.pallas_call(
        functools.partial(pack_kernel, slots),
        out_shape=pltpu.VMEM((devices, 3 * rows, HD), jnp.bfloat16),
        in_specs=[VMEM] * 3,
        out_specs=VMEM,
    )(*local)
    arrived = lax.all_to_all(packed, axes, split_axis=0, concat_axis=0, tiled=True)
    group = max(1, BLOCK // rows)
    size = group * rows
    plan = (devices, rows, spatial_here, group, sizes[1])
    result = pl.pallas_call(
        functools.partial(straight_kernel, plan),
        out_shape=pltpu.VMEM((devices, rows, HD), jnp.bfloat16),
        in_specs=[SMEM, SMEM, VMEM],
        out_specs=VMEM,
        scratch_shapes=[
            pltpu.VMEM((2, devices // group, size, size), jnp.float32),
            pltpu.VMEM((size, HD), jnp.float32),
            pltpu.VMEM((size, HD), jnp.float32),
            pltpu.VMEM((size, HD), jnp.float32),
        ],
    )(span_of_frame, active, pltpu.with_memory_space_constraint(arrived, pltpu.VMEM))
    returned = lax.all_to_all(result, axes, split_axis=0, concat_axis=0, tiled=True)
    out = pl.pallas_call(
        functools.partial(unpack_kernel, slots),
        out_shape=jax.ShapeDtypeStruct((rows, width), jnp.bfloat16),
        in_specs=[VMEM],
        out_specs=VMEM,
    )(pltpu.with_memory_space_constraint(returned, pltpu.VMEM))
    return out.reshape(queries.shape)


def shared_pack_kernel(q_ref, k_ref, v_ref, out_ref, local_ref, sems):
    rows = q_ref.shape[0]
    half, kept = rows // 2, rows - rows // 4
    copies = [
        pltpu.make_async_copy(ref, local_ref.at[index], sems.at[index]) for index, ref in enumerate((k_ref, v_ref, q_ref))
    ]
    for copy in copies:
        copy.start()
    slots = []
    for time in range(0, out_ref.shape[0] // 2, 2):
        for place in range(2):
            own, both = time // 2 * 3 + 2 * place, time // 2 * 3 + 1
            slots.append((time * 2 + place, time * 2 + 2 + place, own, both, place))

    def of(index, head, start=0, stop=rows):
        return local_ref[index, start:stop, head * HD : (head + 1) * HD]

    for index in range(2):
        copies[index].wait()
        for first, second, own, both, _ in slots:
            out_ref[first, index * rows : (index + 1) * rows] = of(index, own)
            out_ref[second, index * rows : (index + 1) * rows] = of(index, both)
    copies[2].wait()
    for first, second, own, both, place in slots:
        out_ref[first, 2 * rows :] = of(2, own, 0, kept)
        out_ref[second, 2 * rows : 2 * rows + half] = of(2, both, place * half, (place + 1) * half)
        out_ref[second, 2 * rows + half :] = of(2, own, kept, rows)


def shared_unpack_kernel(in_ref, out_ref):
    rows = out_ref.shape[0]
    half = rows // 2
    for time in range(0, in_ref.shape[0] // 2, 2):
        for place in range(2):
            own, both = time // 2 * 3 + 2 * place, time // 2 * 3 + 1
            out_ref[:, own * HD : (own + 1) * HD] = in_ref[time * 2 + place]
            out_ref[place * half : (place + 1) * half, both * HD : (both + 1) * HD] = in_ref[time * 2 + 2 + place, :half]


def shared_kernel(plan, axes, span_ref, x_ref, rest_ref, out_ref, score_ref, peak_ref, total_ref, sum_ref):
    devices, rows, spatial, group = plan
    my_core, my_place = lax.axis_index(axes[0]) % 2, lax.axis_index(axes[1])
    blocks = devices // group
    size = group * rows
    half = rows // 2
    block_frames = group // 2 * (rows // spatial)
    scale = HD ** (-0.5) * math.log2(math.e)

    def local_frame(row):
        return row // (2 * rows) * (rows // spatial) + row % rows // spatial

    def part(block, place):
        got = x_ref[pl.ds(block * group, group), place * rows : (place + 1) * rows, :]
        return got.reshape(size, HD)

    def fold(values, op):
        got = values[:, :HD]
        for start in range(HD, values.shape[1], HD):
            got = op(got, values[:, start : start + HD])
        return got

    def scores_of(query, other, mine):
        key = part(other, 0)
        scores = lax.dot_general(query, key, (((1,), (1,)), ((), ())), preferred_element_type=jnp.float32)
        if mine is None:
            return scores
        local = local_frame(lax.broadcasted_iota(jnp.int32, (1, size), 1))
        spans = jnp.full((1, size), span_ref[other * block_frames], jnp.int32)
        for frame in range(1, block_frames):
            spans = jnp.where(local == frame, span_ref[other * block_frames + frame], spans)
        pieces = []
        for start in range(0, size, spatial):
            pieces.append(jnp.where(spans <= mine(start), scores[start : start + spatial], -jnp.inf))
        return jnp.concatenate(pieces, axis=0)

    def probs_of(slot, other, peak):
        probs = jnp.exp2(score_ref[slot, other] * scale - peak)
        product = jnp.dot(probs.astype(jnp.bfloat16), part(other, 1), preferred_element_type=jnp.float32)
        return fold(probs, jnp.add), product

    def straight(wide, query_of, mine_of, write):
        tiles = blocks // wide

        def seen(tile):
            return range(min((tile + 1) * wide + 1, blocks))

        def make_scores(tile):
            query, top = query_of(tile), None
            for other in seen(tile):
                scores = scores_of(query, other, mine_of(tile) if other >= tile * wide else None)
                score_ref[tile % 2, other] = scores
                folded = fold(scores, jnp.maximum)
                top = folded if top is None else jnp.maximum(top, folded)
            return jnp.max(top, axis=1, keepdims=True) * scale

        def weigh(tile, peak):
            total = weighed = None
            for other in seen(tile):
                folded, product = probs_of(tile % 2, other, peak)
                total = folded if total is None else total + folded
                weighed = product if weighed is None else weighed + product
            write(tile, (weighed / jnp.sum(total, axis=1, keepdims=True)).astype(jnp.bfloat16))

        peak = make_scores(tiles - 1)
        for tile in range(tiles - 2, -1, -1):
            following = make_scores(tile)
            weigh(tile + 1, peak)
            peak = following
        weigh(0, peak)

    def looped(wide, query_of, mine_of, write):
        for tile in range(blocks // wide):
            query, mine = query_of(tile), mine_of(tile)
            peak_ref[...] = jnp.full_like(peak_ref, -jnp.inf)
            total_ref[...] = jnp.zeros_like(total_ref)
            sum_ref[...] = jnp.zeros_like(sum_ref)

            def score(other, _, query=query, mine=mine):
                scores = scores_of(query, other, mine)
                score_ref[0, other] = scores
                peak_ref[...] = jnp.maximum(peak_ref[...], fold(scores, jnp.maximum))
                return 0

            lax.fori_loop(0, blocks, score, 0)
            peak = jnp.max(peak_ref[...], axis=1, keepdims=True) * scale

            def weigh(other, _, peak=peak):
                folded, product = probs_of(0, other, peak)
                total_ref[...] += folded
                sum_ref[...] += product
                return 0

            lax.fori_loop(0, blocks, weigh, 0)
            write(tile, (sum_ref[...] / jnp.sum(total_ref[...], axis=1, keepdims=True)).astype(jnp.bfloat16))

    def own_query(tile):
        sources = pl.ds(tile * group, group)
        return jnp.concatenate([x_ref[sources, 2 * rows :, :], rest_ref[sources]], axis=1).reshape(size, HD)

    def own_span(tile):
        return lambda start: span_ref[tile * block_frames + local_frame(start)]

    def own_write(tile, result):
        out_ref[pl.ds(tile * group, group)] = result.reshape(group, rows, HD)

    def both_query(tile):
        return x_ref[pl.ds(tile * 2 * group, 2 * group), 2 * rows : 2 * rows + half, :].reshape(size, HD)

    def both_span(tile):
        return lambda start: span_ref[(tile * 2 * group + start // half) // 2 * 2 + my_place]

    def both_write(tile, result):
        out_ref[pl.ds(tile * 2 * group, 2 * group), :half, :] = result.reshape(2 * group, half, HD)

    near = jnp.bool_(True)
    for block in range(blocks - 2):
        near = near & (span_ref[(block + 2) * block_frames] > span_ref[(block + 1) * block_frames - 1])
    for core, roles in enumerate(((1, own_query, own_span, own_write), (2, both_query, both_span, both_write))):
        here = my_core == core
        pl.when(here & near)(functools.partial(straight, *roles))
        pl.when(here & jnp.logical_not(near))(functools.partial(looped, *roles))


def shared(axes, sizes, queries, keys, values, span_of_frame):
    frames_here, spatial_here, width = queries.shape
    rows = frames_here * spatial_here
    devices = math.prod(sizes)
    group = BLOCK // rows
    size = group * rows
    local = [array.reshape(rows, width) for array in (queries, keys, values)]
    kept = rows - rows // 4
    packed = pl.pallas_call(
        shared_pack_kernel,
        out_shape=pltpu.VMEM((devices, 2 * rows + kept, HD), jnp.bfloat16),
        in_specs=[pl.BlockSpec(memory_space=pl.ANY)] * 3,
        out_specs=VMEM,
        scratch_shapes=[pltpu.VMEM((3, rows, width), jnp.bfloat16), pltpu.SemaphoreType.DMA((3,))],
    )(*local)
    arrived = lax.all_to_all(packed, axes, split_axis=0, concat_axis=0, tiled=True)
    across = [(device, device ^ sizes[1]) for device in range(devices)]
    rest = lax.ppermute(arrived[:, 2 * rows + rows // 2 :], axes, across)
    result = pl.pallas_call(
        functools.partial(shared_kernel, (devices, rows, spatial_here, group), axes),
        out_shape=pltpu.VMEM((devices, rows, HD), jnp.bfloat16),
        in_specs=[SMEM, VMEM, VMEM],
        out_specs=VMEM,
        scratch_shapes=[
            pltpu.VMEM((2, devices // group, size, size), jnp.float32),
            pltpu.VMEM((size, HD), jnp.float32),
            pltpu.VMEM((size, HD), jnp.float32),
            pltpu.VMEM((size, HD), jnp.float32),
        ],
    )(
        span_of_frame,
        pltpu.with_memory_space_constraint(arrived, pltpu.VMEM),
        pltpu.with_memory_space_constraint(rest, pltpu.VMEM),
    )
    returned = lax.all_to_all(result, axes, split_axis=0, concat_axis=0, tiled=True)
    out = pl.pallas_call(
        shared_unpack_kernel,
        out_shape=jax.ShapeDtypeStruct((rows, width), jnp.bfloat16),
        in_specs=[VMEM],
        out_specs=VMEM,
    )(pltpu.with_memory_space_constraint(returned, pltpu.VMEM))
    return out.reshape(queries.shape)


def per_device(axes, sizes, queries, keys, values, span_of_frame):
    tokens = math.prod(sizes) * queries.shape[0] * queries.shape[1]
    way = on_chip if tokens <= 16 * BLOCK else general
    frames_here, spatial_here, width = queries.shape
    fits = sizes[1] == 2 and sizes[0] % 2 == 0 and 2 * (width // HD) == 3 * sizes[0] and frames_here == 2
    if way is on_chip and fits and spatial_here % 32 == 0 and BLOCK % (4 * spatial_here) == 0:
        way = shared
    return way(axes, sizes, queries, keys, values, span_of_frame)


def general(axes, sizes, queries, keys, values, span_of_frame):
    frames_here, spatial_here, width = queries.shape
    heads = width // HD
    rows = frames_here * spatial_here
    devices = math.prod(sizes)
    slots = slots_of(heads, devices)
    packed = pl.pallas_call(
        functools.partial(pack_kernel, slots),
        out_shape=jax.ShapeDtypeStruct((devices, 3 * rows, HD), jnp.bfloat16),
        in_specs=[VMEM] * 3,
        out_specs=VMEM,
    )(*(array.reshape(rows, width) for array in (queries, keys, values)))
    arrived = lax.all_to_all(packed, axes, split_axis=0, concat_axis=0, tiled=True)
    me = lax.axis_index(axes)
    active = functools.reduce(jnp.logical_or, [me == slot for slot in slots]).astype(jnp.int32)
    group = max(1, BLOCK // rows)
    size = group * rows
    plan = (devices, rows, spatial_here, group, sizes[1])
    result = pl.pallas_call(
        functools.partial(attend_kernel, plan),
        out_shape=jax.ShapeDtypeStruct((devices, rows, HD), jnp.bfloat16),
        in_specs=[SMEM, SMEM, VMEM],
        out_specs=VMEM,
        scratch_shapes=[
            pltpu.VMEM((devices // group, size, size), jnp.float32),
            pltpu.VMEM((size, HD), jnp.float32),
            pltpu.VMEM((size, HD), jnp.float32),
            pltpu.VMEM((size, HD), jnp.float32),
        ],
    )(span_of_frame, active.reshape(1), arrived)
    returned = lax.all_to_all(result, axes, split_axis=0, concat_axis=0, tiled=True)
    out = pl.pallas_call(
        functools.partial(unpack_kernel, slots),
        out_shape=jax.ShapeDtypeStruct((rows, width), jnp.bfloat16),
        in_specs=[VMEM],
        out_specs=VMEM,
    )(returned)
    return out.reshape(queries.shape)


def solution(mesh):
    axes = ("tm", "space")
    sizes = tuple(mesh.shape[axis] for axis in axes)
    return jax.shard_map(
        functools.partial(per_device, axes, sizes),
        mesh=mesh,
        in_specs=(P("tm", "space", None), P("tm", "space", None), P("tm", "space", None), P()),
        out_specs=P("tm", "space", None),
        check_vma=False,
    )
```

```python
import functools
import math

import jax
import jax.numpy as jnp
from jax import lax
from jax.experimental import pallas as pl
from jax.experimental.pallas import tpu as pltpu
from jax.sharding import PartitionSpec as P

HD = 128
BLOCK = 256
VMEM = pl.BlockSpec(memory_space=pltpu.VMEM)
SMEM = pl.BlockSpec(memory_space=pltpu.SMEM)


def slots_of(heads, devices):
    return [head * devices // heads for head in range(heads)]


def pack_kernel(slots, q_ref, k_ref, v_ref, out_ref):
    rows = q_ref.shape[0]
    for head, slot in enumerate(slots):
        for place, ref in enumerate((q_ref, k_ref, v_ref)):
            out_ref[slot, place * rows : (place + 1) * rows, :] = ref[:, head * HD : (head + 1) * HD]


def unpack_kernel(slots, in_ref, out_ref):
    for head, slot in enumerate(slots):
        out_ref[:, head * HD : (head + 1) * HD] = in_ref[slot]


def attend_loops(plan, span_ref, x_ref, out_ref, score_ref, peak_ref, total_ref, sum_ref):
    sources, rows, spatial, group, per_frames = plan
    blocks = sources // group
    size = group * rows
    frames_dev = rows // spatial
    block_tms = max(1, group // per_frames)
    block_frames = block_tms * frames_dev
    scale = HD ** (-0.5) * math.log2(math.e)

    def first_frame(block):
        return (block * group) // per_frames * frames_dev

    def part(block, place):
        got = x_ref[pl.ds(block * group, group), place * rows : (place + 1) * rows, :]
        return got.reshape(size, HD)

    def spans_along(block, dimension, shape):
        at = lax.broadcasted_iota(jnp.int32, shape, dimension)
        local = (at // rows) // per_frames * frames_dev + (at % rows) // spatial
        base = first_frame(block)
        spans = jnp.full(shape, span_ref[base], jnp.int32)
        for frame in range(1, block_frames):
            spans = jnp.where(local == frame, span_ref[base + frame], spans)
        return spans

    def fold(values, op):
        got = values[:, :HD]
        for start in range(HD, values.shape[1], HD):
            got = op(got, values[:, start : start + HD])
        return got

    def scores_of(query, block):
        key = part(block, 1)
        return lax.dot_general(query, key, (((1,), (1,)), ((), ())), preferred_element_type=jnp.float32)

    def one_block(block, _):
        low = span_ref[first_frame(block)]
        high = span_ref[first_frame(block) + block_frames - 1]
        whole, seen = jnp.int32(0), jnp.int32(0)
        for other in range(blocks):
            start = first_frame(other)
            whole += (span_ref[start + block_frames - 1] <= low).astype(jnp.int32)
            seen += (span_ref[start] <= high).astype(jnp.int32)
        query = part(block, 0)
        peak_ref[...] = jnp.full_like(peak_ref, -jnp.inf)

        def plain(other, _):
            scores = scores_of(query, other)
            score_ref[other] = scores
            peak_ref[...] = jnp.maximum(peak_ref[...], fold(scores, jnp.maximum))
            return 0

        def masked(other, _):
            visible = spans_along(other, 1, (size, size)) <= spans_along(block, 0, (size, size))
            scores = jnp.where(visible, scores_of(query, other), -jnp.inf)
            score_ref[other] = scores
            peak_ref[...] = jnp.maximum(peak_ref[...], fold(scores, jnp.maximum))
            return 0

        lax.fori_loop(0, whole, plain, 0)
        lax.fori_loop(whole, seen, masked, 0)
        peak = jnp.max(peak_ref[...], axis=1, keepdims=True) * scale
        peak_ref[...] = jnp.broadcast_to(peak, peak_ref.shape)
        total_ref[...] = jnp.zeros_like(total_ref)
        sum_ref[...] = jnp.zeros_like(sum_ref)

        def weigh(other, _):
            peaks = jnp.concatenate([peak_ref[...]] * (size // HD), axis=1)
            probs = jnp.exp2(score_ref[other] * scale - peaks)
            total_ref[...] += fold(probs, jnp.add)
            sum_ref[...] += jnp.dot(probs.astype(jnp.bfloat16), part(other, 2), preferred_element_type=jnp.float32)
            return 0

        lax.fori_loop(0, seen, weigh, 0)
        total = jnp.sum(total_ref[...], axis=1, keepdims=True)
        result = (sum_ref[...] / total).astype(jnp.bfloat16)
        out_ref[pl.ds(block * group, group)] = result.reshape(group, rows, HD)
        return 0

    lax.fori_loop(0, blocks, one_block, 0)


def attend_kernel(plan, span_ref, active_ref, *refs):
    @pl.when(active_ref[0] == 1)
    def _():
        attend_loops(plan, span_ref, *refs)


def straight_kernel(plan, span_ref, active_ref, x_ref, out_ref, score_ref, peak_ref, total_ref, sum_ref):
    sources, rows, spatial, group, per_frames = plan
    blocks = sources // group
    size = group * rows
    frames_dev = rows // spatial
    block_frames = max(1, group // per_frames) * frames_dev
    scale = HD ** (-0.5) * math.log2(math.e)

    def first_frame(block):
        return (block * group) // per_frames * frames_dev

    def local_frame(row):
        return (row // rows) // per_frames * frames_dev + (row % rows) // spatial

    def part(block, place):
        return x_ref[block * group : (block + 1) * group, place * rows : (place + 1) * rows, :].reshape(size, HD)

    def fold(values, op):
        got = values[:, :HD]
        for start in range(HD, values.shape[1], HD):
            got = op(got, values[:, start : start + HD])
        return got

    def masked(scores, block, other):
        local = local_frame(lax.broadcasted_iota(jnp.int32, (1, size), 1))
        spans = jnp.full((1, size), span_ref[first_frame(other)], jnp.int32)
        for frame in range(1, block_frames):
            spans = jnp.where(local == frame, span_ref[first_frame(other) + frame], spans)
        pieces = []
        for start in range(0, size, spatial):
            mine = span_ref[first_frame(block) + local_frame(start)]
            pieces.append(jnp.where(spans <= mine, scores[start : start + spatial], -jnp.inf))
        return jnp.concatenate(pieces, axis=0)

    def seen(block):
        return range(min(block + 2, blocks))

    def make_scores(block):
        query, top = part(block, 0), None
        for other in seen(block):
            scores = lax.dot_general(
                query, part(other, 1), (((1,), (1,)), ((), ())), preferred_element_type=jnp.float32
            )
            if other >= block:
                scores = masked(scores, block, other)
            score_ref[block % 2, other] = scores
            folded = fold(scores, jnp.maximum)
            top = folded if top is None else jnp.maximum(top, folded)
        return jnp.max(top, axis=1, keepdims=True) * scale

    def weigh(block, peak):
        total = weighed = None
        for other in seen(block):
            probs = jnp.exp2(score_ref[block % 2, other] * scale - peak)
            folded = fold(probs, jnp.add)
            product = jnp.dot(probs.astype(jnp.bfloat16), part(other, 2), preferred_element_type=jnp.float32)
            total = folded if total is None else total + folded
            weighed = product if weighed is None else weighed + product
        result = weighed / jnp.sum(total, axis=1, keepdims=True)
        out_ref[block * group : (block + 1) * group] = result.astype(jnp.bfloat16).reshape(group, rows, HD)

    near = jnp.bool_(True)
    for block in range(blocks - 2):
        last = first_frame(block) + block_frames - 1
        near = near & (span_ref[first_frame(block + 2)] > span_ref[last])
    active = active_ref[0] == 1

    @pl.when(active & near)
    def _():
        peak = make_scores(0)
        for block in range(1, blocks):
            following = make_scores(block)
            weigh(block - 1, peak)
            peak = following
        weigh(blocks - 1, peak)

    @pl.when(active & jnp.logical_not(near))
    def _():
        attend_loops(plan, span_ref, x_ref, out_ref, score_ref.at[0], peak_ref, total_ref, sum_ref)


def on_chip(axes, sizes, queries, keys, values, span_of_frame):
    frames_here, spatial_here, width = queries.shape
    heads = width // HD
    rows = frames_here * spatial_here
    devices = math.prod(sizes)
    slots = slots_of(heads, devices)
    me = lax.axis_index(axes)
    active = functools.reduce(jnp.logical_or, [me == slot for slot in slots]).astype(jnp.int32)
    local, active = lax.optimization_barrier(
        ([array.reshape(rows, width) for array in (queries, keys, values)], active.reshape(1))
    )
    packed = pl.pallas_call(
        functools.partial(pack_kernel, slots),
        out_shape=pltpu.VMEM((devices, 3 * rows, HD), jnp.bfloat16),
        in_specs=[VMEM] * 3,
        out_specs=VMEM,
    )(*local)
    arrived = lax.all_to_all(packed, axes, split_axis=0, concat_axis=0, tiled=True)
    group = max(1, BLOCK // rows)
    size = group * rows
    plan = (devices, rows, spatial_here, group, sizes[1])
    result = pl.pallas_call(
        functools.partial(straight_kernel, plan),
        out_shape=pltpu.VMEM((devices, rows, HD), jnp.bfloat16),
        in_specs=[SMEM, SMEM, VMEM],
        out_specs=VMEM,
        scratch_shapes=[
            pltpu.VMEM((2, devices // group, size, size), jnp.float32),
            pltpu.VMEM((size, HD), jnp.float32),
            pltpu.VMEM((size, HD), jnp.float32),
            pltpu.VMEM((size, HD), jnp.float32),
        ],
    )(span_of_frame, active, pltpu.with_memory_space_constraint(arrived, pltpu.VMEM))
    returned = lax.all_to_all(result, axes, split_axis=0, concat_axis=0, tiled=True)
    out = pl.pallas_call(
        functools.partial(unpack_kernel, slots),
        out_shape=jax.ShapeDtypeStruct((rows, width), jnp.bfloat16),
        in_specs=[VMEM],
        out_specs=VMEM,
    )(pltpu.with_memory_space_constraint(returned, pltpu.VMEM))
    return out.reshape(queries.shape)


def shared_pack_kernel(q_ref, k_ref, v_ref, out_ref, local_ref, sems):
    rows = q_ref.shape[0]
    half, kept = rows // 2, rows - rows // 4
    copies = [
        pltpu.make_async_copy(ref, local_ref.at[index], sems.at[index]) for index, ref in enumerate((k_ref, v_ref, q_ref))
    ]
    for copy in copies:
        copy.start()
    slots = []
    for time in range(0, out_ref.shape[0] // 2, 2):
        for place in range(2):
            own, both = time // 2 * 3 + 2 * place, time // 2 * 3 + 1
            slots.append((time * 2 + place, time * 2 + 2 + place, own, both, place))

    def of(index, head, start=0, stop=rows):
        return local_ref[index, start:stop, head * HD : (head + 1) * HD]

    for index in range(2):
        copies[index].wait()
        for first, second, own, both, _ in slots:
            out_ref[first, index * rows : (index + 1) * rows] = of(index, own)
            out_ref[second, index * rows : (index + 1) * rows] = of(index, both)
    copies[2].wait()
    for first, second, own, both, place in slots:
        out_ref[first, 2 * rows :] = of(2, own, 0, kept)
        out_ref[second, 2 * rows : 2 * rows + half] = of(2, both, place * half, (place + 1) * half)
        out_ref[second, 2 * rows + half :] = of(2, own, kept, rows)


def shared_unpack_kernel(in_ref, out_ref, sems):
    rows = out_ref.shape[0]
    half = rows // 2
    copies = []
    for time in range(0, in_ref.shape[0] // 2, 2):
        for place in range(2):
            own, both = time // 2 * 3 + 2 * place, time // 2 * 3 + 1
            first, second = time * 2 + place, time * 2 + 2 + place
            own_out = out_ref.at[:, own * HD : (own + 1) * HD]
            both_out = out_ref.at[place * half : (place + 1) * half, both * HD : (both + 1) * HD]
            copies.append(pltpu.make_async_copy(in_ref.at[first], own_out, sems.at[first]))
            copies.append(pltpu.make_async_copy(in_ref.at[second, :half], both_out, sems.at[second]))
    for copy in copies:
        copy.start()
    for copy in copies:
        copy.wait()


def shared_kernel(plan, axes, span_ref, x_ref, rest_ref, out_ref, score_ref, peak_ref, total_ref, sum_ref):
    devices, rows, spatial, group = plan
    my_core, my_place = lax.axis_index(axes[0]) % 2, lax.axis_index(axes[1])
    blocks = devices // group
    size = group * rows
    half = rows // 2
    block_frames = group // 2 * (rows // spatial)
    scale = HD ** (-0.5) * math.log2(math.e)

    def local_frame(row):
        return row // (2 * rows) * (rows // spatial) + row % rows // spatial

    def part(block, place):
        got = x_ref[pl.ds(block * group, group), place * rows : (place + 1) * rows, :]
        return got.reshape(size, HD)

    def fold(values, op):
        got = values[:, :HD]
        for start in range(HD, values.shape[1], HD):
            got = op(got, values[:, start : start + HD])
        return got

    def scores_of(query, other, mine):
        key = part(other, 0)
        scores = lax.dot_general(query, key, (((1,), (1,)), ((), ())), preferred_element_type=jnp.float32)
        if mine is None:
            return scores
        local = local_frame(lax.broadcasted_iota(jnp.int32, (1, size), 1))
        spans = jnp.full((1, size), span_ref[other * block_frames], jnp.int32)
        for frame in range(1, block_frames):
            spans = jnp.where(local == frame, span_ref[other * block_frames + frame], spans)
        pieces = []
        for start in range(0, size, spatial):
            pieces.append(jnp.where(spans <= mine(start), scores[start : start + spatial], -jnp.inf))
        return jnp.concatenate(pieces, axis=0)

    def probs_of(slot, other, peak):
        probs = jnp.exp2(score_ref[slot, other] * scale - peak)
        product = jnp.dot(probs.astype(jnp.bfloat16), part(other, 1), preferred_element_type=jnp.float32)
        return fold(probs, jnp.add), product

    def straight(wide, query_of, mine_of, write):
        tiles = blocks // wide

        def seen(tile):
            return range(min((tile + 1) * wide + 1, blocks))

        def make_scores(tile):
            query, top = query_of(tile), None
            for other in seen(tile):
                scores = scores_of(query, other, mine_of(tile) if other >= tile * wide else None)
                score_ref[tile % 2, other] = scores
                folded = fold(scores, jnp.maximum)
                top = folded if top is None else jnp.maximum(top, folded)
            return jnp.max(top, axis=1, keepdims=True) * scale

        def weigh(tile, peak):
            total = weighed = None
            for other in seen(tile):
                folded, product = probs_of(tile % 2, other, peak)
                total = folded if total is None else total + folded
                weighed = product if weighed is None else weighed + product
            write(tile, (weighed / jnp.sum(total, axis=1, keepdims=True)).astype(jnp.bfloat16))

        peak = make_scores(tiles - 1)
        for tile in range(tiles - 2, -1, -1):
            following = make_scores(tile)
            weigh(tile + 1, peak)
            peak = following
        weigh(0, peak)

    def looped(wide, query_of, mine_of, write):
        for tile in range(blocks // wide):
            query, mine = query_of(tile), mine_of(tile)
            peak_ref[...] = jnp.full_like(peak_ref, -jnp.inf)
            total_ref[...] = jnp.zeros_like(total_ref)
            sum_ref[...] = jnp.zeros_like(sum_ref)

            def score(other, _, query=query, mine=mine):
                scores = scores_of(query, other, mine)
                score_ref[0, other] = scores
                peak_ref[...] = jnp.maximum(peak_ref[...], fold(scores, jnp.maximum))
                return 0

            lax.fori_loop(0, blocks, score, 0)
            peak = jnp.max(peak_ref[...], axis=1, keepdims=True) * scale

            def weigh(other, _, peak=peak):
                folded, product = probs_of(0, other, peak)
                total_ref[...] += folded
                sum_ref[...] += product
                return 0

            lax.fori_loop(0, blocks, weigh, 0)
            write(tile, (sum_ref[...] / jnp.sum(total_ref[...], axis=1, keepdims=True)).astype(jnp.bfloat16))

    def own_query(tile):
        sources = pl.ds(tile * group, group)
        return jnp.concatenate([x_ref[sources, 2 * rows :, :], rest_ref[sources]], axis=1).reshape(size, HD)

    def own_span(tile):
        return lambda start: span_ref[tile * block_frames + local_frame(start)]

    def own_write(tile, result):
        out_ref[pl.ds(tile * group, group)] = result.reshape(group, rows, HD)

    def both_query(tile):
        return x_ref[pl.ds(tile * 2 * group, 2 * group), 2 * rows : 2 * rows + half, :].reshape(size, HD)

    def both_span(tile):
        return lambda start: span_ref[(tile * 2 * group + start // half) // 2 * 2 + my_place]

    def both_write(tile, result):
        out_ref[pl.ds(tile * 2 * group, 2 * group), :half, :] = result.reshape(2 * group, half, HD)

    near = jnp.bool_(True)
    for block in range(blocks - 2):
        near = near & (span_ref[(block + 2) * block_frames] > span_ref[(block + 1) * block_frames - 1])
    for core, roles in enumerate(((1, own_query, own_span, own_write), (2, both_query, both_span, both_write))):
        here = my_core == core
        pl.when(here & near)(functools.partial(straight, *roles))
        pl.when(here & jnp.logical_not(near))(functools.partial(looped, *roles))


def shared(axes, sizes, queries, keys, values, span_of_frame):
    frames_here, spatial_here, width = queries.shape
    rows = frames_here * spatial_here
    devices = math.prod(sizes)
    group = BLOCK // rows
    size = group * rows
    local = [array.reshape(rows, width) for array in (queries, keys, values)]
    kept = rows - rows // 4
    packed = pl.pallas_call(
        shared_pack_kernel,
        out_shape=pltpu.VMEM((devices, 2 * rows + kept, HD), jnp.bfloat16),
        in_specs=[pl.BlockSpec(memory_space=pl.ANY)] * 3,
        out_specs=VMEM,
        scratch_shapes=[pltpu.VMEM((3, rows, width), jnp.bfloat16), pltpu.SemaphoreType.DMA((3,))],
    )(*local)
    arrived = lax.all_to_all(packed, axes, split_axis=0, concat_axis=0, tiled=True)
    across = [(device, device ^ sizes[1]) for device in range(devices)]
    rest = lax.ppermute(arrived[:, 2 * rows + rows // 2 :], axes, across)
    result = pl.pallas_call(
        functools.partial(shared_kernel, (devices, rows, spatial_here, group), axes),
        out_shape=pltpu.VMEM((devices, rows, HD), jnp.bfloat16),
        in_specs=[SMEM, VMEM, VMEM],
        out_specs=VMEM,
        scratch_shapes=[
            pltpu.VMEM((2, devices // group, size, size), jnp.float32),
            pltpu.VMEM((size, HD), jnp.float32),
            pltpu.VMEM((size, HD), jnp.float32),
            pltpu.VMEM((size, HD), jnp.float32),
        ],
    )(
        span_of_frame,
        pltpu.with_memory_space_constraint(arrived, pltpu.VMEM),
        pltpu.with_memory_space_constraint(rest, pltpu.VMEM),
    )
    returned = lax.all_to_all(result, axes, split_axis=0, concat_axis=0, tiled=True)
    out = pl.pallas_call(
        shared_unpack_kernel,
        out_shape=jax.ShapeDtypeStruct((rows, width), jnp.bfloat16),
        in_specs=[VMEM],
        out_specs=pl.BlockSpec(memory_space=pl.ANY),
        scratch_shapes=[pltpu.SemaphoreType.DMA((devices,))],
    )(pltpu.with_memory_space_constraint(returned, pltpu.VMEM))
    return out.reshape(queries.shape)


def per_device(axes, sizes, queries, keys, values, span_of_frame):
    tokens = math.prod(sizes) * queries.shape[0] * queries.shape[1]
    way = on_chip if tokens <= 16 * BLOCK else general
    frames_here, spatial_here, width = queries.shape
    fits = sizes[1] == 2 and sizes[0] % 2 == 0 and 2 * (width // HD) == 3 * sizes[0] and frames_here == 2
    if way is on_chip and fits and spatial_here % 32 == 0 and BLOCK % (4 * spatial_here) == 0:
        way = shared
    return way(axes, sizes, queries, keys, values, span_of_frame)


def general(axes, sizes, queries, keys, values, span_of_frame):
    frames_here, spatial_here, width = queries.shape
    heads = width // HD
    rows = frames_here * spatial_here
    devices = math.prod(sizes)
    slots = slots_of(heads, devices)
    packed = pl.pallas_call(
        functools.partial(pack_kernel, slots),
        out_shape=jax.ShapeDtypeStruct((devices, 3 * rows, HD), jnp.bfloat16),
        in_specs=[VMEM] * 3,
        out_specs=VMEM,
    )(*(array.reshape(rows, width) for array in (queries, keys, values)))
    arrived = lax.all_to_all(packed, axes, split_axis=0, concat_axis=0, tiled=True)
    me = lax.axis_index(axes)
    active = functools.reduce(jnp.logical_or, [me == slot for slot in slots]).astype(jnp.int32)
    group = max(1, BLOCK // rows)
    size = group * rows
    plan = (devices, rows, spatial_here, group, sizes[1])
    result = pl.pallas_call(
        functools.partial(attend_kernel, plan),
        out_shape=jax.ShapeDtypeStruct((devices, rows, HD), jnp.bfloat16),
        in_specs=[SMEM, SMEM, VMEM],
        out_specs=VMEM,
        scratch_shapes=[
            pltpu.VMEM((devices // group, size, size), jnp.float32),
            pltpu.VMEM((size, HD), jnp.float32),
            pltpu.VMEM((size, HD), jnp.float32),
            pltpu.VMEM((size, HD), jnp.float32),
        ],
    )(span_of_frame, active.reshape(1), arrived)
    returned = lax.all_to_all(result, axes, split_axis=0, concat_axis=0, tiled=True)
    out = pl.pallas_call(
        functools.partial(unpack_kernel, slots),
        out_shape=jax.ShapeDtypeStruct((rows, width), jnp.bfloat16),
        in_specs=[VMEM],
        out_specs=VMEM,
    )(returned)
    return out.reshape(queries.shape)


def solution(mesh):
    axes = ("tm", "space")
    sizes = tuple(mesh.shape[axis] for axis in axes)
    return jax.shard_map(
        functools.partial(per_device, axes, sizes),
        mesh=mesh,
        in_specs=(P("tm", "space", None), P("tm", "space", None), P("tm", "space", None), P()),
        out_specs=P("tm", "space", None),
        check_vma=False,
    )
```
